256 devices in a mesh: outer: 16 (over x, y), inner: 16 (over z, core).
Axes of the slice: x: 4, y: 4, z: 8, core: 2. Of those that a mesh axis runs over, the one named last changes fastest.
Arguments:
- queries: bfloat16 [65536, 16, 128], P(('outer', 'inner')), may hold values from -6 to 6
- key_rows: bfloat16 [65536, 16, 128], P(('outer', 'inner')), may hold values from -6 to 6
- value_rows: bfloat16 [65536, 16, 128], P(('outer', 'inner')), may hold values from -6 to 6
- key_scale: bfloat16 [65536, 16], P(('outer', 'inner')), may hold values from 0.5 to 2
- value_scale: bfloat16 [65536, 16], P(('outer', 'inner')), may hold values from 0.5 to 2
- cluster_label: int32 [16, 65536, 1], P(None, ('outer', 'inner')), may hold values from 0 to 127; in each aligned block of 256 rows (0 to 255, 256 to 511, ..., all dimensions but the last counted through in order) at most 4 rows name the same one
Outputs:
- attended: bfloat16 [65536, 16, 128], P(('outer', 'inner'))
The draws below stay inside these ranges and needn't reach their ends.
Inputs may be any that keep to these rules, and one draw needn't show every extreme that they name: `cluster_label`: among the 256 rows of one device for one head, no label occurs more than 4 times, and some label occurs exactly 4 times.
All inputs are finite; a program needn't handle non-finite values.
Results may differ from the reference program's by a relative error of at most 0.0033.
Values may be sent and summed in bfloat16 or wider, within the bound.
No kernel may reach another device: no remote copies, remote signals or barrier semaphores. Data moves between devices by JAX's collectives and lax.ppermute only.
A program may use at most 64 MiB of HBM per device.

```python
import math
import jax
import jax.numpy as jnp
import numpy as np
from jax import lax

HEADS = 16
HEAD = 128
COARSE = 16
FINE = 8
TOK_DEV = 256
CLUSTERS = 128
CAP = 4
TOKENS = 65536
N_OUTER = 16
N_INNER = 16


def draw_vectors(key, fold_tag):
    drawn = jax.random.normal(jax.random.fold_in(key, fold_tag), (TOKENS, HEADS, HEAD), jnp.float32)
    return jnp.clip(drawn, -6.0, 6.0).astype(jnp.bfloat16)


def draw_queries(key, part):
    return draw_vectors(key, 11)


def draw_key_rows(key, part):
    return draw_vectors(key, 13)


def levels(own_key, dims, pieces, low, high):
    gain = 1.0
    for axis_at, blocks in pieces:
        steps = jax.random.uniform(jax.random.fold_in(jax.random.fold_in(own_key, 6), axis_at), (blocks,), jnp.float32, low / len(pieces), high / len(pieces))
        gain = gain * jnp.repeat(jnp.exp(steps), dims[axis_at] // blocks).reshape((-1,) + (1,) * (len(dims) - 1 - axis_at))
    return gain


def routed_block(rng, own, number, rows, amount, top, reach, lean):
    sequence = jax.random.permutation(rng, amount)
    heavy_load, ordinary = shares(amount, rows * top, reach, lean, True), shares(amount, rows * top, reach, lean, False)
    places = jnp.arange(amount)

    def named(sizes, offset_by):
        used = int((sizes > 0).sum())
        fixed = max(1, used // 4)
        shifted = fixed + (places - fixed + offset_by * (used - fixed)) % max(1, amount - fixed)
        return jnp.zeros((amount,), jnp.int32).at[sequence[jnp.where(places < fixed, places, shifted)]].set(jnp.asarray(sizes, jnp.int32))

    sizes = jnp.where(number % 4 == 0, named(heavy_load, number // 4), named(ordinary, number - number // 4 - 1))
    mixed = jax.random.permutation(jax.random.fold_in(own, 3), amount)
    donor, receiver = mixed[0:amount // 2 * 2:2], mixed[1:amount // 2 * 2:2]
    margin = jnp.minimum(sizes[donor] - 1, reach - sizes[receiver]) // 2
    margin = jnp.where((donor == sequence[0]) | (receiver == sequence[0]) | (sizes[receiver] == 0), 0, jnp.maximum(margin, 0))
    shifted = jax.random.randint(jax.random.fold_in(own, 4), (amount // 2,), 0, 1 << 20) % (margin + 1)
    sizes = sizes.at[donor].add(-shifted).at[receiver].add(shifted)
    items = jnp.searchsorted(jnp.cumsum(sizes), jnp.arange(rows * top), side="right").astype(jnp.int32)
    table = items.reshape(top, rows).T
    table = table[jax.random.permutation(jax.random.fold_in(own, 1), rows)]
    offset_by = jax.random.randint(jax.random.fold_in(own, 2), (rows, 1), 0, top)
    return jnp.take_along_axis(table, (jnp.arange(top)[None, :] + offset_by) % top, axis=1)


def shares(count, total, most, slope, full):
    loads = [(1 << 20) // math.isqrt(rank ** slope) + 1 for rank in range(1, count + 1)]
    largest = most if full else min(most, max(-(-total // count), total * loads[0] // sum(loads)))
    least = 1 if total - largest >= count - 1 else 0
    holding, spare = [largest] + [least] * (count - 1), total - largest - least * (count - 1)
    while spare > 0:
        free = [i for i in range(1, count) if holding[i] < largest] or [i for i in range(1, count) if holding[i] < most]
        mass, budget = sum([loads[i] for i in free]), spare
        for i in free:
            addition = min(most - holding[i], max(1, budget * loads[i] // mass), spare)
            holding[i] = holding[i] + addition
            spare = spare - addition
    return np.array(holding)


def noise(rng, dims, scale, reach, split=(), kind=jnp.bfloat16):
    loudness = levels(rng, dims, split, -0.22, 0.18) if split else 1.0
    values = jax.random.normal(rng, dims, jnp.float32) * scale * loudness
    return jnp.minimum(jnp.maximum(values, -reach), reach).astype(kind)


def setup_inputs(seed: int = 0) -> dict:
    arg_keys = jax.random.split(jax.random.key(seed), 7)
    queries = draw_queries(jax.random.fold_in(arg_keys[6], 71), 0)
    key_rows = draw_key_rows(jax.random.fold_in(arg_keys[6], 71), 0)
    value_rows = noise(arg_keys[2], (TOKENS, HEADS, HEAD), 1.0, 6.0, ((0, 256),))
    key_scale = jnp.clip(jnp.exp(math.log(2.0) - 1.3862944 * jax.random.uniform(arg_keys[3], (TOKENS, HEADS), jnp.float32) ** levels(arg_keys[3], (TOKENS, HEADS), ((0, 256),), -0.2, 0.2)), 0.5, 2.0).astype(jnp.bfloat16)
    value_scale = jnp.clip(jnp.exp(math.log(2.0) - 1.3862944 * jax.random.uniform(arg_keys[4], (TOKENS, HEADS), jnp.float32) ** levels(arg_keys[4], (TOKENS, HEADS), ((0, 256),), -0.2, 0.2)), 0.5, 2.0).astype(jnp.bfloat16)
    cluster_label_keys = jax.random.split(jax.random.fold_in(arg_keys[5], 1), HEADS * TOKENS // TOK_DEV)
    cluster_label_turns = jax.random.permutation(jax.random.fold_in(arg_keys[5], 3), HEADS * TOKENS // TOK_DEV)
    cluster_label = jax.vmap(lambda own, number: routed_block(jax.random.fold_in(arg_keys[5], 2), own, number, TOK_DEV, CLUSTERS, 1, CAP, 2))(cluster_label_keys, cluster_label_turns).reshape((HEADS, TOKENS, 1))
    return dict(queries=queries, key_rows=key_rows, value_rows=value_rows, key_scale=key_scale, value_scale=value_scale, cluster_label=cluster_label)


def attend(query_block, key_block, value_block, key_factor, value_factor, position):
    factor = query_block.shape[-1] ** -0.5
    scores = jnp.dot(query_block, key_block.T, preferred_element_type=jnp.float32)
    scores = scores * (key_factor.astype(jnp.float32) * factor)[None, :]
    visible = (position[None, :] >= 0) & (position[None, :] <= position[:, None])
    highest = jnp.max(jnp.where(visible, scores, jnp.float32(-1e30)), axis=1, keepdims=True)
    unnormed = jnp.where(visible, jnp.exp(scores - highest), jnp.float32(0.0))
    denominator = jnp.sum(unnormed, axis=1)
    weights = (unnormed * value_factor.astype(jnp.float32)[None, :]).astype(jnp.bfloat16)
    numerator = jnp.dot(weights, value_block, preferred_element_type=jnp.float32)
    safe = jnp.where(denominator > 0, denominator, jnp.float32(1.0))
    return (numerator / safe[:, None]).astype(jnp.bfloat16)


def reference(queries, key_rows, value_rows, key_scale, value_scale, cluster_label):
    cluster_count = COARSE * FINE
    window = N_OUTER * N_INNER * CAP
    token_count = queries.shape[0]
    width = queries.shape[2]

    def per_head(inputs):
        query_head, key_head, value_head, key_factor, value_factor, labels = inputs
        order = jnp.argsort(labels, stable=True).astype(jnp.int32)
        counts = jnp.zeros((cluster_count,), jnp.int32).at[labels].add(1)
        starts = jnp.cumsum(counts) - counts

        def per_cluster(which):
            offset = jnp.arange(window, dtype=jnp.int32)
            inside = offset < counts[which]
            token = order[jnp.minimum(starts[which] + offset, token_count - 1)]
            position = jnp.where(inside, token, -1).astype(jnp.int32)
            result = attend(query_head[token], key_head[token], value_head[token],
                            key_factor[token], value_factor[token], position)
            target = jnp.where(inside, token, token_count).astype(jnp.int32)
            return result, target

        results, targets = lax.map(per_cluster, jnp.arange(cluster_count, dtype=jnp.int32))
        empty = jnp.zeros((token_count, width), jnp.bfloat16)
        return empty.at[targets.reshape(-1)].set(results.reshape(-1, width), mode="drop")

    stacked = lax.map(per_head, (jnp.swapaxes(queries, 0, 1), jnp.swapaxes(key_rows, 0, 1),
                                 jnp.swapaxes(value_rows, 0, 1), key_scale.T, value_scale.T,
                                 cluster_label[:, :, 0]))
    return jnp.swapaxes(stacked, 0, 1)
```

```python
import jax
import jax.numpy as jnp
from jax import lax
from jax.experimental import pallas as pl
from jax.experimental.pallas import tpu as pltpu
from jax.sharding import PartitionSpec as P

COARSE = 16
FINE = 8
CAP = 4
CLUSTERS = COARSE * FINE
SLOTS = CLUSTERS * CAP
CHUNK = FINE * CAP
BOTH = ("outer", "inner")
NT = (((1,), (1,)), ((), ()))
NEG = -1e30
LOG2E = 1.4426950408889634


def iota(shape, axis):
    return lax.broadcasted_iota(jnp.int32, shape, axis)


def one_hot(condition):
    return jnp.where(condition, 1.0, 0.0).astype(jnp.bfloat16)


def matmul(a, b):
    return jnp.dot(a, b, preferred_element_type=jnp.float32)


def matmul_nt(a, b):
    return lax.dot_general(a, b, NT, preferred_element_type=jnp.float32)


def swap_matrix(major, minor, unit):
    total = major * minor * unit
    row, column = iota((total, total), 0), iota((total, total), 1)
    b, a, u = row // (major * unit), (row // unit) % major, row % unit
    return one_hot(column == (a * minor + b) * unit + u)


def slots_kernel(label_ref, key_scale_ref, value_scale_ref, slot_ref, scale_ref):
    heads, rows = label_ref.shape
    eye = one_hot(iota((heads, heads), 0) == iota((heads, heads), 1))
    key_rows = matmul_nt(eye, key_scale_ref[...])
    value_rows = matmul_nt(eye, value_scale_ref[...])
    before = one_hot(iota((rows, rows), 0) < iota((rows, rows), 1))
    for h in range(heads):
        label = label_ref[h : h + 1, :]
        member = iota((CLUSTERS, rows), 0) == label
        count = matmul(one_hot(member), before)
        rank = jnp.sum(jnp.where(member, count, 0.0), axis=0, keepdims=True).astype(jnp.int32)
        slot_ref[h : h + 1, :] = label * CAP + rank
        coarse = one_hot(iota((COARSE, rows), 0) == label // FINE)
        here = iota((CHUNK, rows), 0) == (label % FINE) * CAP + rank
        scales = jnp.concatenate(
            [
                jnp.where(here, key_rows[h : h + 1, :], 0.0),
                jnp.where(here, value_rows[h : h + 1, :], 0.0),
                jnp.zeros((128 - 2 * CHUNK, rows), jnp.float32),
            ],
            axis=0,
        ).astype(jnp.bfloat16)
        scale_ref[pl.ds(h, COARSE, stride=heads), :] = matmul_nt(coarse, scales)


HALF = 8


def place_kernel(slot_ref, q_ref, k_ref, v_ref, out_ref, by_head):
    step = pl.program_id(0)
    rows, _, width = q_ref.shape
    group = 256 // HALF
    swap = swap_matrix(group, HALF, 1)
    for a, ref in enumerate((q_ref, k_ref, v_ref)):
        for g in range(rows // group):
            block = ref[g * group : (g + 1) * group].reshape(256, width)
            turned = matmul(swap, block).astype(jnp.bfloat16).reshape(HALF, group, width)
            by_head[:, g * group : (g + 1) * group, a * width : (a + 1) * width] = turned
    for h in range(HALF):
        slot = slot_ref[pl.ds(step * HALF + h, 1), :]
        pick = one_hot(iota((SLOTS, rows), 0) == slot)
        placed = matmul(pick, by_head[h]).astype(jnp.bfloat16)
        for a in range(3):
            out_ref[:, h, a * CHUNK : (a + 1) * CHUNK, :] = placed[
                :, a * width : (a + 1) * width
            ].reshape(COARSE, CHUNK, width)


def attend_kernel(message_ref, scale_ref, out_ref, qs, ks, vs, os, scales):
    f = pl.program_id(0)
    sources, _, width = message_ref.shape
    total = sources * CAP
    batch = 256 // CHUNK
    unit = batch * CAP

    @pl.when(f == 0)
    def _():
        swap = swap_matrix(batch, FINE, CAP)

        @pl.loop(0, sources // batch)
        def _(g):
            for a, ref in enumerate((qs, ks, vs)):
                block = message_ref[pl.ds(g * batch, batch), a * CHUNK : (a + 1) * CHUNK, :]
                turned = matmul(swap, block.reshape(256, width)).astype(jnp.bfloat16)
                ref[:, pl.ds(pl.multiple_of(g * unit, unit), unit), :] = turned.reshape(
                    FINE, unit, width
                )

        spread = one_hot(iota((total, sources), 0) // CAP == iota((total, sources), 1))
        table = matmul(spread, scale_ref[...].astype(jnp.bfloat16))
        lane, row = iota((total, 128), 1), iota((total, 128), 0)
        table = jnp.where(lane % CAP == row % CAP, table, 0.0).astype(jnp.bfloat16)
        gather = one_hot(iota((2 * FINE, 128), 0) == iota((2 * FINE, 128), 1) // CAP)
        scales[...] = matmul_nt(gather, table)

    key_scale = scales[pl.ds(f, 1), :]
    value_scale = scales[pl.ds(FINE + f, 1), :]
    factor = key_scale * (width**-0.5 * LOG2E)
    bias = jnp.where(key_scale > 0.0, 0.0, NEG)
    tile = 256
    ahead = iota((tile, tile), 1) > iota((tile, tile), 0)
    for t in range(total // tile):
        here = slice(t * tile, (t + 1) * tile)
        query = qs[f, here, :]
        pieces = []
        for u in range(t + 1):
            there = slice(u * tile, (u + 1) * tile)
            score = matmul_nt(query, ks[f, there, :])
            score = score * factor[:, there] + bias[:, there]
            if u == t:
                score = jnp.where(ahead, NEG, score)
            pieces.append(score)
        highest = pieces[0]
        for piece in pieces[1:]:
            highest = jnp.maximum(highest, piece)
        highest = jnp.max(highest, axis=1, keepdims=True)
        below, result = None, None
        for u, piece in enumerate(pieces):
            there = slice(u * tile, (u + 1) * tile)
            unnormed = jnp.exp2(piece - highest)
            weights = (unnormed * value_scale[:, there]).astype(jnp.bfloat16)
            term = matmul(weights, vs[f, there, :])
            below = unnormed if below is None else below + unnormed
            result = term if result is None else result + term
        below = jnp.sum(below, axis=1, keepdims=True)
        os[f, here, :] = (result / below).astype(jnp.bfloat16)

    @pl.when(f == FINE - 1)
    def _():
        swap = swap_matrix(FINE, batch, CAP)

        @pl.loop(0, sources // batch)
        def _(g):
            block = os[:, pl.ds(pl.multiple_of(g * unit, unit), unit), :].reshape(256, width)
            turned = matmul(swap, block).astype(jnp.bfloat16)
            out_ref[pl.ds(g * batch, batch)] = turned.reshape(batch, CHUNK, width)


def unplace_kernel(slot_ref, in_ref, out_ref, by_head):
    step = pl.program_id(0)
    rows = slot_ref.shape[0]
    width = in_ref.shape[3]
    group = 256 // HALF
    swap = swap_matrix(HALF, group, 1)
    lane = iota(slot_ref.shape, 1)
    for h in range(HALF):
        slot = jnp.sum(
            jnp.where(lane == step * HALF + h, slot_ref[...], 0), axis=1, keepdims=True
        )
        pick = one_hot(iota((rows, SLOTS), 1) == slot)
        by_head[h] = matmul(pick, in_ref[:, h].reshape(SLOTS, width)).astype(jnp.bfloat16)
    for g in range(rows // group):
        block = by_head[:, g * group : (g + 1) * group, :].reshape(256, width)
        out_ref[g * group : (g + 1) * group] = (
            matmul(swap, block).astype(jnp.bfloat16).reshape(group, HALF, width)
        )


def shards(queries, key_rows, value_rows, key_scale, value_scale, cluster_label):
    rows, heads, width = queries.shape
    devices = lax.axis_size("outer") * lax.axis_size("inner")
    labels = cluster_label.reshape(heads, rows)
    bf16, f32 = jnp.bfloat16, jnp.float32
    slots, scales = pl.pallas_call(
        slots_kernel,
        out_shape=(
            jax.ShapeDtypeStruct((heads, rows), jnp.int32),
            jax.ShapeDtypeStruct((COARSE * heads, 128), f32),
        ),
        cost_estimate=pl.CostEstimate(flops=10**8, bytes_accessed=10**6, transcendentals=0),
    )(labels, key_scale, value_scale)
    scales = lax.all_to_all(scales.reshape(devices, 1, 128), BOTH, 0, 0, tiled=True)
    scales = scales.reshape(devices, 128)

    tokens = pl.BlockSpec((rows, HALF, width), lambda i: (0, i, 0))
    message = pl.pallas_call(
        place_kernel,
        grid=(heads // HALF,),
        in_specs=[pl.BlockSpec((heads, rows), lambda i: (0, 0)), tokens, tokens, tokens],
        out_specs=pl.BlockSpec((COARSE, HALF, 3 * CHUNK, width), lambda i: (0, i, 0, 0)),
        out_shape=jax.ShapeDtypeStruct((COARSE, heads, 3 * CHUNK, width), bf16),
        scratch_shapes=[pltpu.VMEM((HALF, rows, 3 * width), bf16)],
        cost_estimate=pl.CostEstimate(
            flops=3 * 10**9, bytes_accessed=9 * 2**20, transcendentals=0
        ),
    )(slots, queries, key_rows, value_rows)
    message = message.reshape(devices, 3 * CHUNK, width)
    message = lax.all_to_all(message, BOTH, 0, 0, tiled=True)

    total = devices * CAP
    table = pltpu.VMEM((FINE, total, width), bf16)
    answer = pl.pallas_call(
        attend_kernel,
        grid=(FINE,),
        in_specs=[
            pl.BlockSpec((devices, 3 * CHUNK, width), lambda i: (0, 0, 0)),
            pl.BlockSpec((devices, 128), lambda i: (0, 0)),
        ],
        out_specs=pl.BlockSpec((devices, CHUNK, width), lambda i: (0, 0, 0)),
        out_shape=jax.ShapeDtypeStruct((devices, CHUNK, width), bf16),
        scratch_shapes=[table, table, table, table, pltpu.VMEM((2 * FINE, total), f32)],
        cost_estimate=pl.CostEstimate(
            flops=4 * 10**9, bytes_accessed=8 * 2**20, transcendentals=5 * 10**6
        ),
    )(message, scales)
    answer = lax.all_to_all(answer, BOTH, 0, 0, tiled=True)

    return pl.pallas_call(
        unplace_kernel,
        grid=(heads // HALF,),
        in_specs=[
            pl.BlockSpec((rows, heads), lambda i: (0, 0)),
            pl.BlockSpec((COARSE, HALF, CHUNK, width), lambda i: (0, i, 0, 0)),
        ],
        out_specs=pl.BlockSpec((rows, HALF, width), lambda i: (0, i, 0)),
        out_shape=jax.ShapeDtypeStruct((rows, heads, width), bf16),
        scratch_shapes=[pltpu.VMEM((HALF, rows, width), bf16)],
        cost_estimate=pl.CostEstimate(
            flops=10**9, bytes_accessed=3 * 2**20, transcendentals=0
        ),
    )(slots.T, answer.reshape(COARSE, heads, CHUNK, width))


def solution(mesh):
    placed = (
        P(BOTH, None, None),
        P(BOTH, None, None),
        P(BOTH, None, None),
        P(BOTH, None),
        P(BOTH, None),
        P(None, BOTH, None),
    )
    return jax.shard_map(
        shards,
        mesh=mesh,
        in_specs=placed,
        out_specs=P(BOTH, None, None),
        check_vma=False,
    )
```

```python
import jax
import jax.numpy as jnp
from jax import lax
from jax.experimental import pallas as pl
from jax.experimental.pallas import tpu as pltpu
from jax.sharding import PartitionSpec as P

COARSE = 16
FINE = 8
CAP = 4
CLUSTERS = COARSE * FINE
SLOTS = CLUSTERS * CAP
CHUNK = FINE * CAP
META = 8
BOTH = ("outer", "inner")
NT = (((1,), (1,)), ((), ()))
NEG = -1e30
LOG2E = 1.4426950408889634
HALF = 8


def iota(shape, axis):
    return lax.broadcasted_iota(jnp.int32, shape, axis)


def one_hot(condition):
    return jnp.where(condition, 1.0, 0.0).astype(jnp.bfloat16)


def matmul(a, b):
    return jnp.dot(a, b, preferred_element_type=jnp.float32)


def matmul_nt(a, b):
    return lax.dot_general(a, b, NT, preferred_element_type=jnp.float32)


def swap_matrix(major, minor, unit):
    total = major * minor * unit
    row, column = iota((total, total), 0), iota((total, total), 1)
    b, a, u = row // (major * unit), (row // unit) % major, row % unit
    return one_hot(column == (a * minor + b) * unit + u)


def pack_kernel(label_ref, key_scale_ref, value_scale_ref, q_ref, slot_ref, out_ref):
    rows, heads, width = q_ref.shape
    before = one_hot(iota((rows, rows), 0) < iota((rows, rows), 1))
    for h in range(heads):
        label = label_ref[h]
        member = iota((CLUSTERS, rows), 0) == label
        count = matmul(one_hot(member), before)
        rank = jnp.sum(jnp.where(member, count, 0.0), axis=0, keepdims=True).astype(jnp.int32)
        slot = label * CAP + rank
        slot_ref[h : h + 1, :] = slot
        kinds = (
            (slot // CHUNK).astype(jnp.float32),
            (slot % CHUNK).astype(jnp.float32),
            key_scale_ref[h : h + 1, :].astype(jnp.float32),
            value_scale_ref[h : h + 1, :].astype(jnp.float32),
        )
        meta = jnp.concatenate(
            [kind[:, half : half + width] for kind in kinds for half in range(0, rows, width)],
            axis=0,
        )
        out_ref[h, rows : rows + META, :] = meta.astype(jnp.bfloat16)
    group = 256 // heads
    swap = swap_matrix(group, heads, 1)
    for g in range(rows // group):
        block = q_ref[g * group : (g + 1) * group].reshape(256, width)
        turned = matmul(swap, block).astype(jnp.bfloat16)
        out_ref[:, g * group : (g + 1) * group, :] = turned.reshape(heads, group, width)


def place_kernel(slot_ref, k_ref, v_ref, out_ref, by_head):
    step = pl.program_id(0)
    rows, _, width = k_ref.shape
    group = 256 // HALF
    swap = swap_matrix(group, HALF, 1)
    for g in range(rows // group):
        here = slice(g * group, (g + 1) * group)
        block = jnp.concatenate(
            [k_ref[here].reshape(256, width), v_ref[here].reshape(256, width)], axis=1
        )
        turned = matmul(swap, block).astype(jnp.bfloat16)
        by_head[:, here, :] = turned.reshape(HALF, group, 2 * width)
    for h in range(HALF):
        slot = slot_ref[pl.ds(step * HALF + h, 1), :]
        pick = one_hot(iota((SLOTS, rows), 0) == slot)
        placed = matmul(pick, by_head[h]).astype(jnp.bfloat16)
        out_ref[:, h] = placed.reshape(COARSE, CHUNK, 2 * width)


def sort_kernel(me_ref, in_ref, *refs):
    outs, (table, scales) = refs[:COARSE], refs[COARSE:]
    me = me_ref[0]
    blocks, rows, width = in_ref.shape
    rows = rows - META
    batch = 256 // CHUNK
    for s in range(blocks):
        meta = in_ref[s, rows : rows + META, :].astype(jnp.float32)
        coarse, here, key_scale, value_scale = (
            jnp.concatenate([meta[2 * n : 2 * n + 1], meta[2 * n + 1 : 2 * n + 2]], axis=1)
            for n in range(4)
        )
        owner = coarse.astype(jnp.int32) ^ me
        here = here.astype(jnp.int32)
        pick = one_hot(iota((SLOTS, rows), 0) == owner * CHUNK + here)
        placed = matmul(pick, in_ref[s, :rows, :]).astype(jnp.bfloat16)
        table[:, s] = placed.reshape(COARSE, CHUNK, width)
        mine = iota((CHUNK, rows), 0) == here
        both = jnp.concatenate(
            [
                jnp.where(mine, key_scale, 0.0),
                jnp.where(mine, value_scale, 0.0),
                jnp.zeros((width - 2 * CHUNK, rows), jnp.float32),
            ],
            axis=0,
        ).astype(jnp.bfloat16)
        scales[pl.ds(s, COARSE, stride=blocks), :] = matmul_nt(
            one_hot(iota((COARSE, rows), 0) == owner), both
        )
    swap = swap_matrix(batch, FINE, CAP)
    unit = batch * CAP
    for d, out_ref in enumerate(outs):
        block = jnp.concatenate(
            [
                table[d, b * batch : (b + 1) * batch].reshape(256, width)
                for b in range(blocks // batch)
            ],
            axis=1,
        )
        turned = matmul(swap, block).astype(jnp.bfloat16)
        for f in range(FINE):
            for b in range(blocks // batch):
                at = f * blocks * CAP + b * unit
                out_ref[at : at + unit, :] = turned[
                    f * unit : (f + 1) * unit, b * width : (b + 1) * width
                ]
        out_ref[FINE * blocks * CAP :, :] = scales[d * blocks : (d + 1) * blocks, :].astype(
            jnp.bfloat16
        )


def attend_kernel(me_ref, message_ref, *refs):
    parts, out_ref = refs[:COARSE], refs[COARSE]
    qs, kvs, os, scale_rows, scales = refs[COARSE + 1 :]
    f = pl.program_id(0)
    sources, _, width = message_ref.shape
    width = width // 2
    blocks = sources // COARSE
    total = sources * CAP
    batch = 256 // CHUNK
    unit = batch * CAP
    slab = blocks * CAP

    @pl.when(f == 0)
    def _():
        me = me_ref[0]
        for d, part in enumerate(parts):
            source = me ^ d
            qs[:, pl.ds(pl.multiple_of(source * slab, slab), slab), :] = part[
                : FINE * slab, :
            ].reshape(FINE, slab, width)
            scale_rows[pl.ds(pl.multiple_of(source * blocks, blocks), blocks), :] = part[
                FINE * slab :, :
            ]
        swap = swap_matrix(batch, FINE, CAP)

        def turn(g, carry):
            block = message_ref[pl.ds(g * batch, batch)].reshape(256, 2 * width)
            turned = matmul(swap, block).astype(jnp.bfloat16)
            kvs[:, pl.ds(pl.multiple_of(g * unit, unit), unit), :] = turned.reshape(
                FINE, unit, 2 * width
            )
            return carry

        lax.fori_loop(0, sources // batch, turn, 0, unroll=8)

        spread = one_hot(iota((total, sources), 0) // CAP == iota((total, sources), 1))
        table = matmul(spread, scale_rows[...])
        lane, row = iota((total, 128), 1), iota((total, 128), 0)
        table = jnp.where(lane % CAP == row % CAP, table, 0.0).astype(jnp.bfloat16)
        gather = one_hot(iota((2 * FINE, 128), 0) == iota((2 * FINE, 128), 1) // CAP)
        scales[...] = matmul_nt(gather, table)

    key_scale = scales[pl.ds(f, 1), :]
    value_scale = scales[pl.ds(FINE + f, 1), :]
    factor = key_scale * (width**-0.5 * LOG2E)
    bias = jnp.where(key_scale > 0.0, 0.0, NEG)
    tile = 256
    ahead = iota((tile, tile), 1) > iota((tile, tile), 0)
    for t in range(total // tile):
        here = slice(t * tile, (t + 1) * tile)
        query = qs[f, here, :]
        pieces = []
        for u in range(t + 1):
            there = slice(u * tile, (u + 1) * tile)
            score = matmul_nt(query, kvs[f, there, :width])
            score = score * factor[:, there] + bias[:, there]
            if u == t:
                score = jnp.where(ahead, NEG, score)
            pieces.append(score)
        highest = pieces[0]
        for piece in pieces[1:]:
            highest = jnp.maximum(highest, piece)
        highest = jnp.max(highest, axis=1, keepdims=True)
        below, result = None, None
        for u, piece in enumerate(pieces):
            there = slice(u * tile, (u + 1) * tile)
            unnormed = jnp.exp2(piece - highest)
            weights = (unnormed * value_scale[:, there]).astype(jnp.bfloat16)
            term = matmul(weights, kvs[f, there, width:])
            below = unnormed if below is None else below + unnormed
            result = term if result is None else result + term
        below = jnp.sum(below, axis=1, keepdims=True)
        os[f, here, :] = (result / below).astype(jnp.bfloat16)

    @pl.when(f == FINE - 1)
    def _():
        swap = swap_matrix(FINE, batch, CAP)

        def turn(g, carry):
            block = os[:, pl.ds(pl.multiple_of(g * unit, unit), unit), :].reshape(256, width)
            turned = matmul(swap, block).astype(jnp.bfloat16)
            out_ref[pl.ds(g * batch, batch)] = turned.reshape(batch, CHUNK, width)
            return carry

        lax.fori_loop(0, sources // batch, turn, 0, unroll=8)


def unplace_kernel(slot_ref, in_ref, out_ref, by_head):
    step = pl.program_id(0)
    rows = slot_ref.shape[0]
    width = in_ref.shape[3]
    group = 256 // HALF
    swap = swap_matrix(HALF, group, 1)
    lane = iota(slot_ref.shape, 1)
    for h in range(HALF):
        slot = jnp.sum(
            jnp.where(lane == step * HALF + h, slot_ref[...], 0), axis=1, keepdims=True
        )
        pick = one_hot(iota((rows, SLOTS), 1) == slot)
        by_head[h] = matmul(pick, in_ref[:, h].reshape(SLOTS, width)).astype(jnp.bfloat16)
    for g in range(rows // group):
        block = by_head[:, g * group : (g + 1) * group, :].reshape(256, width)
        out_ref[g * group : (g + 1) * group] = (
            matmul(swap, block).astype(jnp.bfloat16).reshape(group, HALF, width)
        )


def shards(queries, key_rows, value_rows, key_scale, value_scale, cluster_label):
    rows, heads, width = queries.shape
    outer, inner = lax.axis_size("outer"), lax.axis_size("inner")
    devices = outer * inner
    bf16, f32 = jnp.bfloat16, jnp.float32
    me = lax.axis_index("outer").astype(jnp.int32).reshape(1)
    scalar = pl.BlockSpec(memory_space=pltpu.SMEM)

    slots, packed = pl.pallas_call(
        pack_kernel,
        out_shape=(
            jax.ShapeDtypeStruct((heads, rows), jnp.int32),
            jax.ShapeDtypeStruct((heads, rows + META, width), bf16),
        ),
        cost_estimate=pl.CostEstimate(flops=10**9, bytes_accessed=2**21, transcendentals=0),
    )(jnp.swapaxes(cluster_label, 1, 2), key_scale.T, value_scale.T, queries)
    packed = lax.all_to_all(packed, "inner", 0, 0, tiled=True)

    tokens = pl.BlockSpec((rows, HALF, width), lambda i: (0, i, 0))
    message = pl.pallas_call(
        place_kernel,
        grid=(heads // HALF,),
        in_specs=[pl.BlockSpec((heads, rows), lambda i: (0, 0)), tokens, tokens],
        out_specs=pl.BlockSpec((COARSE, HALF, CHUNK, 2 * width), lambda i: (0, i, 0, 0)),
        out_shape=jax.ShapeDtypeStruct((COARSE, heads, CHUNK, 2 * width), bf16),
        scratch_shapes=[pltpu.VMEM((HALF, rows, 2 * width), bf16)],
        cost_estimate=pl.CostEstimate(
            flops=3 * 10**9, bytes_accessed=6 * 2**20, transcendentals=0
        ),
    )(slots, key_rows, value_rows)
    message = message.reshape(devices, CHUNK, 2 * width)
    message = lax.all_to_all(message, BOTH, 0, 0, tiled=True)

    part_rows = FINE * inner * CAP + inner
    parts = pl.pallas_call(
        sort_kernel,
        in_specs=[scalar, pl.BlockSpec(memory_space=pltpu.VMEM)],
        out_shape=[jax.ShapeDtypeStruct((part_rows, width), bf16)] * COARSE,
        scratch_shapes=[
            pltpu.VMEM((COARSE, inner, CHUNK, width), bf16),
            pltpu.VMEM((COARSE * inner, width), f32),
        ],
        cost_estimate=pl.CostEstimate(
            flops=2 * 10**9, bytes_accessed=3 * 2**20, transcendentals=0
        ),
    )(me, packed)
    parts = [parts[0]] + [
        lax.ppermute(parts[d], "outer", [(n, n ^ d) for n in range(outer)])
        for d in range(1, outer)
    ]

    total = devices * CAP
    answer = pl.pallas_call(
        attend_kernel,
        grid=(FINE,),
        in_specs=[scalar, pl.BlockSpec((devices, CHUNK, 2 * width), lambda i: (0, 0, 0))]
        + [pl.BlockSpec((part_rows, width), lambda i: (0, 0))] * COARSE,
        out_specs=pl.BlockSpec((devices, CHUNK, width), lambda i: (0, 0, 0)),
        out_shape=jax.ShapeDtypeStruct((devices, CHUNK, width), bf16),
        scratch_shapes=[
            pltpu.VMEM((FINE, total, width), bf16),
            pltpu.VMEM((FINE, total, 2 * width), bf16),
            pltpu.VMEM((FINE, total, width), bf16),
            pltpu.VMEM((devices, width), bf16),
            pltpu.VMEM((2 * FINE, total), f32),
        ],
        cost_estimate=pl.CostEstimate(
            flops=4 * 10**9, bytes_accessed=8 * 2**20, transcendentals=5 * 10**6
        ),
    )(me, message, *parts)
    answer = lax.all_to_all(answer, BOTH, 0, 0, tiled=True)

    return pl.pallas_call(
        unplace_kernel,
        grid=(heads // HALF,),
        in_specs=[
            pl.BlockSpec((rows, heads), lambda i: (0, 0)),
            pl.BlockSpec((COARSE, HALF, CHUNK, width), lambda i: (0, i, 0, 0)),
        ],
        out_specs=pl.BlockSpec((rows, HALF, width), lambda i: (0, i, 0)),
        out_shape=jax.ShapeDtypeStruct((rows, heads, width), bf16),
        scratch_shapes=[pltpu.VMEM((HALF, rows, width), bf16)],
        cost_estimate=pl.CostEstimate(
            flops=10**9, bytes_accessed=3 * 2**20, transcendentals=0
        ),
    )(slots.T, answer.reshape(COARSE, heads, CHUNK, width))


def solution(mesh):
    placed = (
        P(BOTH, None, None),
        P(BOTH, None, None),
        P(BOTH, None, None),
        P(BOTH, None),
        P(BOTH, None),
        P(None, BOTH, None),
    )
    return jax.shard_map(
        shards,
        mesh=mesh,
        in_specs=placed,
        out_specs=P(BOTH, None, None),
        check_vma=False,
    )
```

```python
import jax
import jax.numpy as jnp
from jax import lax
from jax.experimental import pallas as pl
from jax.experimental.pallas import tpu as pltpu
from jax.sharding import PartitionSpec as P

COARSE = 16
FINE = 8
CAP = 4
CLUSTERS = COARSE * FINE
SLOTS = CLUSTERS * CAP
CHUNK = FINE * CAP
META = 8
BOTH = ("outer", "inner")
NT = (((1,), (1,)), ((), ()))
NEG = -1e30
LOG2E = 1.4426950408889634
HALF = 8


def iota(shape, axis):
    return lax.broadcasted_iota(jnp.int32, shape, axis)


def one_hot(condition):
    return jnp.where(condition, 1.0, 0.0).astype(jnp.bfloat16)


def matmul(a, b):
    return jnp.dot(a, b, preferred_element_type=jnp.float32)


def matmul_nt(a, b):
    return lax.dot_general(a, b, NT, preferred_element_type=jnp.float32)


def swap_matrix(major, minor, unit):
    total = major * minor * unit
    row, column = iota((total, total), 0), iota((total, total), 1)
    b, a, u = row // (major * unit), (row // unit) % major, row % unit
    return one_hot(column == (a * minor + b) * unit + u)


def slot_of(label, before):
    member = iota((CLUSTERS, label.shape[1]), 0) == label
    count = matmul(one_hot(member), before)
    rank = jnp.sum(jnp.where(member, count, 0.0), axis=0, keepdims=True)
    return label * CAP + rank.astype(jnp.int32)


def before_matrix(rows):
    return one_hot(iota((rows, rows), 0) < iota((rows, rows), 1))


def pack_kernel(label_ref, key_scale_ref, value_scale_ref, q_ref, out_ref):
    rows, heads, width = q_ref.shape
    halves = rows // width
    for h in range(heads):
        kinds = (
            label_ref[h].astype(jnp.float32),
            key_scale_ref[h : h + 1, :].astype(jnp.float32),
            value_scale_ref[h : h + 1, :].astype(jnp.float32),
        )
        meta = jnp.concatenate(
            [kind[:, n * width : (n + 1) * width] for kind in kinds for n in range(halves)]
            + [jnp.zeros((META - 3 * halves, width), jnp.float32)],
            axis=0,
        )
        out_ref[h, rows : rows + META, :] = meta.astype(jnp.bfloat16)
    group = 256 // heads
    swap = swap_matrix(group, heads, 1)
    for g in range(rows // group):
        block = q_ref[g * group : (g + 1) * group].reshape(256, width)
        turned = matmul(swap, block).astype(jnp.bfloat16)
        out_ref[:, g * group : (g + 1) * group, :] = turned.reshape(heads, group, width)


def place_kernel(label_ref, k_ref, v_ref, slot_ref, out_ref, by_head):
    rows, _, width = k_ref.shape
    group = 256 // HALF
    swap = swap_matrix(group, HALF, 1)
    for g in range(rows // group):
        here = slice(g * group, (g + 1) * group)
        block = jnp.concatenate(
            [k_ref[here].reshape(256, width), v_ref[here].reshape(256, width)], axis=1
        )
        turned = matmul(swap, block).astype(jnp.bfloat16)
        by_head[:, here, :] = turned.reshape(HALF, group, 2 * width)
    before = before_matrix(rows)
    for h in range(HALF):
        slot = slot_of(label_ref[h], before)
        slot_ref[h : h + 1, :] = slot
        pick = one_hot(iota((SLOTS, rows), 0) == slot)
        placed = matmul(pick, by_head[h]).astype(jnp.bfloat16)
        out_ref[:, h] = placed.reshape(COARSE, CHUNK, 2 * width)


def sort_kernel(me_ref, arrived_ref, *refs):
    outs, (table, scales, in_ref, sems) = refs[:COARSE], refs[COARSE:]
    me = me_ref[0]
    blocks, rows, width = in_ref.shape
    rows = rows - META
    batch = 256 // CHUNK
    quarter = blocks // 4
    copies = [
        pltpu.make_async_copy(
            arrived_ref.at[pl.ds(n * quarter, quarter)],
            in_ref.at[pl.ds(n * quarter, quarter)],
            sems.at[n],
        )
        for n in range(4)
    ]
    for copy in copies:
        copy.start()
    before = before_matrix(rows)
    for s in range(blocks):
        if s % quarter == 0:
            copies[s // quarter].wait()
        meta = in_ref[s, rows : rows + META, :].astype(jnp.float32)
        label, key_scale, value_scale = (
            jnp.concatenate([meta[2 * n : 2 * n + 1], meta[2 * n + 1 : 2 * n + 2]], axis=1)
            for n in range(3)
        )
        slot = slot_of(label.astype(jnp.int32), before)
        owner = (slot // CHUNK) ^ me
        here = slot % CHUNK
        pick = one_hot(iota((SLOTS, rows), 0) == owner * CHUNK + here)
        placed = matmul(pick, in_ref[s, :rows, :]).astype(jnp.bfloat16)
        table[:, s] = placed.reshape(COARSE, CHUNK, width)
        mine = iota((CHUNK, rows), 0) == here
        both = jnp.concatenate(
            [
                jnp.where(mine, key_scale, 0.0),
                jnp.where(mine, value_scale, 0.0),
                jnp.zeros((width - 2 * CHUNK, rows), jnp.float32),
            ],
            axis=0,
        ).astype(jnp.bfloat16)
        scales[pl.ds(s, COARSE, stride=blocks), :] = matmul_nt(
            one_hot(iota((COARSE, rows), 0) == owner), both
        )
    swap = swap_matrix(batch, FINE, CAP)
    unit = batch * CAP
    for d, out_ref in enumerate(outs):
        block = jnp.concatenate(
            [
                table[d, b * batch : (b + 1) * batch].reshape(256, width)
                for b in range(blocks // batch)
            ],
            axis=1,
        )
        turned = matmul(swap, block).astype(jnp.bfloat16)
        for f in range(FINE):
            for b in range(blocks // batch):
                at = f * blocks * CAP + b * unit
                out_ref[at : at + unit, :] = turned[
                    f * unit : (f + 1) * unit, b * width : (b + 1) * width
                ]
        out_ref[FINE * blocks * CAP :, :] = scales[d * blocks : (d + 1) * blocks, :].astype(
            jnp.bfloat16
        )


def queries_kernel(me_ref, *refs):
    parts, (qs, scales, scale_rows) = refs[:COARSE], refs[COARSE:]
    me = me_ref[0]
    total, width = qs.shape[1:]
    sources = total // CAP
    blocks = sources // COARSE
    slab = blocks * CAP
    for d, part in enumerate(parts):
        source = me ^ d
        qs[:, pl.ds(pl.multiple_of(source * slab, slab), slab), :] = part[
            : FINE * slab, :
        ].reshape(FINE, slab, width)
        scale_rows[pl.ds(pl.multiple_of(source * blocks, blocks), blocks), :] = part[
            FINE * slab :, :
        ]
    spread = one_hot(iota((total, sources), 0) // CAP == iota((total, sources), 1))
    table = matmul(spread, scale_rows[...])
    lane, row = iota((total, 128), 1), iota((total, 128), 0)
    table = jnp.where(lane % CAP == row % CAP, table, 0.0).astype(jnp.bfloat16)
    gather = one_hot(iota((2 * FINE, 128), 0) == iota((2 * FINE, 128), 1) // CAP)
    scales[...] = matmul_nt(gather, table)


PIECES = 4


def attend_kernel(arrived_ref, qs, scales, out_ref, message, kvs, os, sems):
    f = pl.program_id(0)
    sources, _, width = message.shape
    width = width // 2
    total = sources * CAP
    batch = 256 // CHUNK
    unit = batch * CAP

    @pl.when(f == 0)
    def _():
        piece = sources // PIECES
        copies = [
            pltpu.make_async_copy(
                arrived_ref.at[pl.ds(n * piece, piece)],
                message.at[pl.ds(n * piece, piece)],
                sems.at[n],
            )
            for n in range(PIECES)
        ]
        for copy in copies:
            copy.start()
        swap = swap_matrix(batch, FINE, CAP)
        for n in range(PIECES):
            copies[n].wait()
            for g in range(n * piece // batch, (n + 1) * piece // batch):
                block = message[g * batch : (g + 1) * batch].reshape(256, 2 * width)
                turned = matmul(swap, block).astype(jnp.bfloat16)
                kvs[:, g * unit : (g + 1) * unit, :] = turned.reshape(FINE, unit, 2 * width)

    key_scale = scales[pl.ds(f, 1), :]
    value_scale = scales[pl.ds(FINE + f, 1), :]
    factor = key_scale * (width**-0.5 * LOG2E)
    bias = jnp.where(key_scale > 0.0, 0.0, NEG)
    tile = 256
    ahead = iota((tile, tile), 1) > iota((tile, tile), 0)
    for t in range(total // tile):
        here = slice(t * tile, (t + 1) * tile)
        query = qs[0, here, :]
        pieces = []
        for u in range(t + 1):
            there = slice(u * tile, (u + 1) * tile)
            score = matmul_nt(query, kvs[f, there, :width])
            score = score * factor[:, there] + bias[:, there]
            if u == t:
                score = jnp.where(ahead, NEG, score)
            pieces.append(score)
        highest = pieces[0]
        for piece in pieces[1:]:
            highest = jnp.maximum(highest, piece)
        highest = jnp.max(highest, axis=1, keepdims=True)
        below, result = None, None
        for u, piece in enumerate(pieces):
            there = slice(u * tile, (u + 1) * tile)
            unnormed = jnp.exp2(piece - highest)
            weights = (unnormed * value_scale[:, there]).astype(jnp.bfloat16)
            term = matmul(weights, kvs[f, there, width:])
            below = unnormed if below is None else below + unnormed
            result = term if result is None else result + term
        below = jnp.sum(below, axis=1, keepdims=True)
        os[f, here, :] = (result / below).astype(jnp.bfloat16)

    @pl.when(f == FINE - 1)
    def _():
        swap = swap_matrix(FINE, batch, CAP)

        def turn(g, carry):
            block = os[:, pl.ds(pl.multiple_of(g * unit, unit), unit), :].reshape(256, width)
            turned = matmul(swap, block).astype(jnp.bfloat16)
            out_ref[pl.ds(g * batch, batch)] = turned.reshape(batch, CHUNK, width)
            return carry

        lax.fori_loop(0, sources // batch, turn, 0, unroll=8)


def unplace_kernel(slot_ref, arrived_ref, out_ref, by_head, answer, sems):
    step = pl.program_id(0)
    rows = slot_ref.shape[0]
    width = out_ref.shape[2]

    def copy(n):
        return pltpu.make_async_copy(
            arrived_ref.at[:, pl.ds(n * HALF, HALF)], answer.at[n], sems.at[n]
        )

    @pl.when(step == 0)
    def _():
        for n in range(answer.shape[0]):
            copy(n).start()

    copy(step).wait()
    in_ref = answer.at[step]
    group = 256 // HALF
    swap = swap_matrix(HALF, group, 1)
    lane = iota(slot_ref.shape, 1)
    for h in range(HALF):
        slot = jnp.sum(
            jnp.where(lane == step * HALF + h, slot_ref[...], 0), axis=1, keepdims=True
        )
        pick = one_hot(iota((rows, SLOTS), 1) == slot)
        by_head[h] = matmul(pick, in_ref[:, h].reshape(SLOTS, width)).astype(jnp.bfloat16)
    for g in range(rows // group):
        block = by_head[:, g * group : (g + 1) * group, :].reshape(256, width)
        out_ref[g * group : (g + 1) * group] = (
            matmul(swap, block).astype(jnp.bfloat16).reshape(group, HALF, width)
        )


def shards(queries, key_rows, value_rows, key_scale, value_scale, cluster_label):
    rows, heads, width = queries.shape
    outer, inner = lax.axis_size("outer"), lax.axis_size("inner")
    devices = outer * inner
    bf16, f32 = jnp.bfloat16, jnp.float32
    me = lax.axis_index("outer").astype(jnp.int32).reshape(1)
    scalar = pl.BlockSpec(memory_space=pltpu.SMEM)

    anywhere = pl.BlockSpec(memory_space=pl.ANY)
    labels = jnp.swapaxes(cluster_label, 1, 2)
    packed = pl.pallas_call(
        pack_kernel,
        out_shape=jax.ShapeDtypeStruct((heads, rows + META, width), bf16),
        cost_estimate=pl.CostEstimate(flops=10**9, bytes_accessed=2**21, transcendentals=0),
    )(labels, key_scale.T, value_scale.T, queries)
    packed = lax.all_to_all(packed, "inner", 0, 0, tiled=True)

    tokens = pl.BlockSpec((rows, HALF, width), lambda i: (0, i, 0))
    slots, message = pl.pallas_call(
        place_kernel,
        grid=(heads // HALF,),
        in_specs=[pl.BlockSpec((HALF, 1, rows), lambda i: (i, 0, 0)), tokens, tokens],
        out_specs=[
            pl.BlockSpec((HALF, rows), lambda i: (i, 0)),
            pl.BlockSpec((COARSE, HALF, CHUNK, 2 * width), lambda i: (0, i, 0, 0)),
        ],
        out_shape=[
            jax.ShapeDtypeStruct((heads, rows), jnp.int32),
            jax.ShapeDtypeStruct((COARSE, heads, CHUNK, 2 * width), bf16),
        ],
        scratch_shapes=[pltpu.VMEM((HALF, rows, 2 * width), bf16)],
        cost_estimate=pl.CostEstimate(
            flops=3 * 10**9, bytes_accessed=6 * 2**20, transcendentals=0
        ),
    )(labels, key_rows, value_rows)
    message = message.reshape(devices, CHUNK, 2 * width)
    message = lax.all_to_all(message, BOTH, 0, 0, tiled=True)

    part_rows = FINE * inner * CAP + inner
    parts = pl.pallas_call(
        sort_kernel,
        in_specs=[scalar, anywhere],
        out_shape=[jax.ShapeDtypeStruct((part_rows, width), bf16)] * COARSE,
        scratch_shapes=[
            pltpu.VMEM((COARSE, inner, CHUNK, width), bf16),
            pltpu.VMEM((COARSE * inner, width), f32),
            pltpu.VMEM((inner, rows + META, width), bf16),
            pltpu.SemaphoreType.DMA((4,)),
        ],
        compiler_params=pltpu.CompilerParams(vmem_limit_bytes=24 * 2**20),
        cost_estimate=pl.CostEstimate(
            flops=2 * 10**9, bytes_accessed=3 * 2**20, transcendentals=0
        ),
    )(me, packed)
    parts = [parts[0]] + [
        lax.ppermute(parts[d], "outer", [(n, n ^ d) for n in range(outer)])
        for d in range(1, outer)
    ]

    total = devices * CAP
    by_cluster, scales = pl.pallas_call(
        queries_kernel,
        in_specs=[scalar] + [pl.BlockSpec(memory_space=pltpu.VMEM)] * COARSE,
        out_shape=[
            jax.ShapeDtypeStruct((FINE, total, width), bf16),
            jax.ShapeDtypeStruct((2 * FINE, total), f32),
        ],
        scratch_shapes=[pltpu.VMEM((devices, width), bf16)],
        cost_estimate=pl.CostEstimate(
            flops=10**9, bytes_accessed=4 * 2**20, transcendentals=0
        ),
    )(me, *parts)
    answer = pl.pallas_call(
        attend_kernel,
        grid=(FINE,),
        in_specs=[
            anywhere,
            pl.BlockSpec((1, total, width), lambda i: (i, 0, 0)),
            pl.BlockSpec((2 * FINE, total), lambda i: (0, 0)),
        ],
        out_specs=pl.BlockSpec((devices, CHUNK, width), lambda i: (0, 0, 0)),
        out_shape=jax.ShapeDtypeStruct((devices, CHUNK, width), bf16),
        scratch_shapes=[
            pltpu.VMEM((devices, CHUNK, 2 * width), bf16),
            pltpu.VMEM((FINE, total, 2 * width), bf16),
            pltpu.VMEM((FINE, total, width), bf16),
            pltpu.SemaphoreType.DMA((PIECES,)),
        ],
        cost_estimate=pl.CostEstimate(
            flops=4 * 10**9, bytes_accessed=8 * 2**20, transcendentals=5 * 10**6
        ),
    )(message, by_cluster, scales)
    answer = lax.all_to_all(answer, BOTH, 0, 0, tiled=True)

    return pl.pallas_call(
        unplace_kernel,
        grid=(heads // HALF,),
        in_specs=[
            pl.BlockSpec((rows, heads), lambda i: (0, 0)),
            anywhere,
        ],
        out_specs=pl.BlockSpec((rows, HALF, width), lambda i: (0, i, 0)),
        out_shape=jax.ShapeDtypeStruct((rows, heads, width), bf16),
        scratch_shapes=[
            pltpu.VMEM((HALF, rows, width), bf16),
            pltpu.VMEM((heads // HALF, COARSE, HALF, CHUNK, width), bf16),
            pltpu.SemaphoreType.DMA((heads // HALF,)),
        ],
        compiler_params=pltpu.CompilerParams(vmem_limit_bytes=24 * 2**20),
        cost_estimate=pl.CostEstimate(
            flops=10**9, bytes_accessed=3 * 2**20, transcendentals=0
        ),
    )(slots.T, answer.reshape(COARSE, heads, CHUNK, width))


def solution(mesh):
    placed = (
        P(BOTH, None, None),
        P(BOTH, None, None),
        P(BOTH, None, None),
        P(BOTH, None),
        P(BOTH, None),
        P(None, BOTH, None),
    )
    return jax.shard_map(
        shards,
        mesh=mesh,
        in_specs=placed,
        out_specs=P(BOTH, None, None),
        check_vma=False,
    )
```

```python
import jax
import jax.numpy as jnp
from jax import lax
from jax.experimental import pallas as pl
from jax.experimental.pallas import tpu as pltpu
from jax.sharding import PartitionSpec as P

COARSE = 16
FINE = 8
CAP = 4
CLUSTERS = COARSE * FINE
SLOTS = CLUSTERS * CAP
CHUNK = FINE * CAP
META = 8
BOTH = ("outer", "inner")
NT = (((1,), (1,)), ((), ()))
NEG = -1e30
LOG2E = 1.4426950408889634
HALF = 8
PIECES = 4


def iota(shape, axis):
    return lax.broadcasted_iota(jnp.int32, shape, axis)


def one_hot(condition):
    return jnp.where(condition, 1.0, 0.0).astype(jnp.bfloat16)


def matmul(a, b):
    return jnp.dot(a, b, preferred_element_type=jnp.float32)


def matmul_nt(a, b):
    return lax.dot_general(a, b, NT, preferred_element_type=jnp.float32)


def over(x, size):
    return x >> (size.bit_length() - 1)


def rest(x, size):
    return x & (size - 1)


def swap_matrix(major, minor, unit):
    total = major * minor * unit
    row, column = iota((total, total), 0), iota((total, total), 1)
    b, a, u = over(row, major * unit), rest(over(row, unit), major), rest(row, unit)
    return one_hot(column == (a * minor + b) * unit + u)


def slot_of(label, before):
    member = iota((CLUSTERS, label.shape[1]), 0) == label
    count = matmul(one_hot(member), before)
    rank = jnp.sum(jnp.where(member, count, 0.0), axis=0, keepdims=True)
    return label * CAP + rank.astype(jnp.int32)


def before_matrix(rows):
    return one_hot(iota((rows, rows), 0) < iota((rows, rows), 1))


def pack_kernel(label_ref, key_scale_ref, value_scale_ref, q_ref, out_ref):
    rows, heads, width = q_ref.shape
    kinds = (label_ref[:, 0, :].astype(jnp.float32), key_scale_ref[...], value_scale_ref[...])
    meta = [
        kind[:, n * width : (n + 1) * width].astype(jnp.bfloat16)
        for kind in kinds
        for n in range(rows // width)
    ]
    meta.append(jnp.zeros(((META - len(meta)) * heads, width), jnp.bfloat16))
    turned = matmul(swap_matrix(META, heads, 1), jnp.concatenate(meta, axis=0))
    out_ref[:, rows : rows + META, :] = turned.astype(jnp.bfloat16).reshape(heads, META, width)
    group = 256 // heads
    swap = swap_matrix(group, heads, 1)
    for g in range(rows // group):
        block = q_ref[g * group : (g + 1) * group].reshape(256, width)
        turned = matmul(swap, block).astype(jnp.bfloat16)
        out_ref[:, g * group : (g + 1) * group, :] = turned.reshape(heads, group, width)


def place_kernel(label_ref, k_ref, v_ref, slot_ref, out_ref, by_head):
    rows, _, width = k_ref.shape
    group = 256 // HALF
    swap = swap_matrix(group, HALF, 1)
    for g in range(rows // group):
        here = slice(g * group, (g + 1) * group)
        block = jnp.concatenate(
            [k_ref[here].reshape(256, width), v_ref[here].reshape(256, width)], axis=1
        )
        turned = matmul(swap, block).astype(jnp.bfloat16)
        by_head[:, here, :] = turned.reshape(HALF, group, 2 * width)
    before = before_matrix(rows)
    for h in range(HALF):
        slot = slot_of(label_ref[h], before)
        slot_ref[h : h + 1, :] = slot
        pick = one_hot(iota((SLOTS, rows), 0) == slot)
        placed = matmul(pick, by_head[h]).astype(jnp.bfloat16)
        out_ref[:, h] = placed.reshape(COARSE, CHUNK, 2 * width)


def sort_kernel(me_ref, arrived_ref, *refs):
    outs, (table, scales, in_ref, sems) = refs[:COARSE], refs[COARSE:]
    me = me_ref[0]
    blocks, rows, width = in_ref.shape
    rows = rows - META
    batch = 256 // CHUNK
    quarter = blocks // 4
    copies = [
        pltpu.make_async_copy(
            arrived_ref.at[pl.ds(n * quarter, quarter)],
            in_ref.at[pl.ds(n * quarter, quarter)],
            sems.at[n],
        )
        for n in range(4)
    ]
    for copy in copies:
        copy.start()
    before = before_matrix(rows)
    for s in range(blocks):
        if s % quarter == 0:
            copies[s // quarter].wait()
        meta = in_ref[s, rows : rows + META, :].astype(jnp.float32)
        label, key_scale, value_scale = (
            jnp.concatenate([meta[2 * n : 2 * n + 1], meta[2 * n + 1 : 2 * n + 2]], axis=1)
            for n in range(3)
        )
        slot = slot_of(label.astype(jnp.int32), before)
        owner = over(slot, CHUNK) ^ me
        here = rest(slot, CHUNK)
        pick = one_hot(iota((SLOTS, rows), 0) == owner * CHUNK + here)
        placed = matmul(pick, in_ref[s, :rows, :]).astype(jnp.bfloat16)
        table[:, s] = placed.reshape(COARSE, CHUNK, width)
        mine = iota((CHUNK, rows), 0) == here
        both = jnp.concatenate(
            [
                jnp.where(mine, key_scale, 0.0),
                jnp.where(mine, value_scale, 0.0),
                jnp.zeros((width - 2 * CHUNK, rows), jnp.float32),
            ],
            axis=0,
        ).astype(jnp.bfloat16)
        scales[pl.ds(s, COARSE, stride=blocks), :] = matmul_nt(
            one_hot(iota((COARSE, rows), 0) == owner), both
        )
    swap = swap_matrix(batch, FINE, CAP)
    unit = batch * CAP
    for d, out_ref in enumerate(outs):
        block = jnp.concatenate(
            [
                table[d, b * batch : (b + 1) * batch].reshape(256, width)
                for b in range(blocks // batch)
            ],
            axis=1,
        )
        turned = matmul(swap, block).astype(jnp.bfloat16)
        for f in range(FINE):
            for b in range(blocks // batch):
                at = f * blocks * CAP + b * unit
                out_ref[at : at + unit, :] = turned[
                    f * unit : (f + 1) * unit, b * width : (b + 1) * width
                ]
        out_ref[FINE * blocks * CAP :, :] = scales[d * blocks : (d + 1) * blocks, :].astype(
            jnp.bfloat16
        )


def queries_kernel(me_ref, *refs):
    parts, (qs, scales, scale_rows) = refs[:COARSE], refs[COARSE:]
    me = me_ref[0]
    total, width = qs.shape[1:]
    sources = total // CAP
    blocks = sources // COARSE
    slab = blocks * CAP
    for d, part in enumerate(parts):
        source = me ^ d
        qs[:, pl.ds(pl.multiple_of(source * slab, slab), slab), :] = part[
            : FINE * slab, :
        ].reshape(FINE, slab, width)
        scale_rows[pl.ds(pl.multiple_of(source * blocks, blocks), blocks), :] = part[
            FINE * slab :, :
        ]
    spread = one_hot(over(iota((total, sources), 0), CAP) == iota((total, sources), 1))
    table = matmul(spread, scale_rows[...])
    lane, row = iota((total, 128), 1), iota((total, 128), 0)
    table = jnp.where(rest(lane, CAP) == rest(row, CAP), table, 0.0).astype(jnp.bfloat16)
    gather = one_hot(iota((2 * FINE, 128), 0) == over(iota((2 * FINE, 128), 1), CAP))
    scales[...] = matmul_nt(gather, table)


def attend_kernel(arrived_ref, q_ref, scales, out_ref, message, qs, kvs, os, result, sems):
    sources, _, width = message.shape
    width = width // 2
    piece = sources // PIECES
    tile = piece * CAP
    batch = 256 // CHUNK
    unit = batch * CAP

    def rows(n, size):
        return slice(n * size, (n + 1) * size)

    def message_in(n):
        here = pl.ds(n * piece, piece)
        return pltpu.make_async_copy(arrived_ref.at[here], message.at[here], sems.at[0, n])

    def queries_in(n):
        here = pl.ds(n * tile, tile)
        return pltpu.make_async_copy(q_ref.at[:, here], qs.at[:, here], sems.at[1, n])

    def result_out(n):
        here = pl.ds(n * piece, piece)
        return pltpu.make_async_copy(result.at[here], out_ref.at[here], sems.at[2, n])

    for n in range(PIECES):
        message_in(n).start()
        queries_in(n).start()
    turn_in = swap_matrix(batch, FINE, CAP)
    turn_out = swap_matrix(FINE, batch, CAP)
    ahead = iota((tile, tile), 1) > iota((tile, tile), 0)
    for t in range(PIECES):
        message_in(t).wait()
        for g in range(t * piece // batch, (t + 1) * piece // batch):
            block = message[rows(g, batch)].reshape(256, 2 * width)
            turned = matmul(turn_in, block).astype(jnp.bfloat16)
            kvs[:, rows(g, unit), :] = turned.reshape(FINE, unit, 2 * width)
        queries_in(t).wait()

        def one(f, carry):
            key_scale = scales[pl.ds(f, 1), :]
            value_scale = scales[pl.ds(FINE + f, 1), :]
            factor = key_scale * (width**-0.5 * LOG2E)
            bias = jnp.where(key_scale > 0.0, 0.0, NEG)
            query = qs[f, rows(t, tile), :]
            pieces = []
            for u in range(t + 1):
                there = rows(u, tile)
                score = matmul_nt(query, kvs[f, there, :width])
                score = score * factor[:, there] + bias[:, there]
                if u == t:
                    score = jnp.where(ahead, NEG, score)
                pieces.append(score)
            highest = pieces[0]
            for score in pieces[1:]:
                highest = jnp.maximum(highest, score)
            highest = jnp.max(highest, axis=1, keepdims=True)
            below, total = None, None
            for u, score in enumerate(pieces):
                there = rows(u, tile)
                unnormed = jnp.exp2(score - highest)
                weights = (unnormed * value_scale[:, there]).astype(jnp.bfloat16)
                term = matmul(weights, kvs[f, there, width:])
                below = unnormed if below is None else below + unnormed
                total = term if total is None else total + term
            below = jnp.sum(below, axis=1, keepdims=True)
            os[f] = (total / below).astype(jnp.bfloat16)
            return carry

        lax.fori_loop(0, FINE, one, 0, unroll=FINE)
        for g in range(piece // batch):
            block = os[:, rows(g, unit), :].reshape(256, width)
            turned = matmul(turn_out, block).astype(jnp.bfloat16)
            result[rows(t * (piece // batch) + g, batch)] = turned.reshape(batch, CHUNK, width)
        result_out(t).start()
    for n in range(PIECES):
        result_out(n).wait()


def unplace_kernel(slot_ref, arrived_ref, out_ref, answer, by_head, result, sems):
    rows, heads, width = result.shape
    some = heads // PIECES
    piece = rows // PIECES
    group = 256 // heads

    def answer_in(n):
        here = pl.ds(n * some, some)
        return pltpu.make_async_copy(
            arrived_ref.at[:, here], answer.at[:, here], sems.at[0, n]
        )

    def result_out(n):
        here = pl.ds(n * piece, piece)
        return pltpu.make_async_copy(result.at[here], out_ref.at[here], sems.at[1, n])

    for n in range(PIECES):
        answer_in(n).start()
    place = iota((rows, SLOTS), 1)
    swap = swap_matrix(heads, group, 1)
    for h in range(heads):
        if h % some == 0:
            answer_in(h // some).wait()
        pick = one_hot(place == slot_ref[:, h : h + 1])
        block = answer[:, h].reshape(SLOTS, width)
        by_head[h] = matmul(pick, block).astype(jnp.bfloat16)
    for n in range(PIECES):
        for g in range(n * piece // group, (n + 1) * piece // group):
            here = slice(g * group, (g + 1) * group)
            block = by_head[:, here, :].reshape(256, width)
            result[here] = matmul(swap, block).astype(jnp.bfloat16).reshape(group, heads, width)
        result_out(n).start()
    for n in range(PIECES):
        result_out(n).wait()


def shards(queries, key_rows, value_rows, key_scale, value_scale, cluster_label):
    rows, heads, width = queries.shape
    outer, inner = lax.axis_size("outer"), lax.axis_size("inner")
    devices = outer * inner
    bf16, f32 = jnp.bfloat16, jnp.float32
    me = lax.axis_index("outer").astype(jnp.int32).reshape(1)
    scalar = pl.BlockSpec(memory_space=pltpu.SMEM)

    anywhere = pl.BlockSpec(memory_space=pl.ANY)
    labels = jnp.swapaxes(cluster_label, 1, 2)
    packed = pl.pallas_call(
        pack_kernel,
        out_shape=jax.ShapeDtypeStruct((heads, rows + META, width), bf16),
        cost_estimate=pl.CostEstimate(flops=10**9, bytes_accessed=2**21, transcendentals=0),
    )(labels, key_scale.T, value_scale.T, queries)
    packed = lax.all_to_all(packed, "inner", 0, 0, tiled=True)

    tokens = pl.BlockSpec((rows, HALF, width), lambda i: (0, i, 0))
    slots, message = pl.pallas_call(
        place_kernel,
        grid=(heads // HALF,),
        in_specs=[pl.BlockSpec((HALF, 1, rows), lambda i: (i, 0, 0)), tokens, tokens],
        out_specs=[
            pl.BlockSpec((HALF, rows), lambda i: (i, 0)),
            pl.BlockSpec((COARSE, HALF, CHUNK, 2 * width), lambda i: (0, i, 0, 0)),
        ],
        out_shape=[
            jax.ShapeDtypeStruct((heads, rows), jnp.int32),
            jax.ShapeDtypeStruct((COARSE, heads, CHUNK, 2 * width), bf16),
        ],
        scratch_shapes=[pltpu.VMEM((HALF, rows, 2 * width), bf16)],
        cost_estimate=pl.CostEstimate(
            flops=3 * 10**9, bytes_accessed=6 * 2**20, transcendentals=0
        ),
    )(labels, key_rows, value_rows)
    message = message.reshape(devices, CHUNK, 2 * width)
    message = lax.all_to_all(message, BOTH, 0, 0, tiled=True)

    part_rows = FINE * inner * CAP + inner
    parts = pl.pallas_call(
        sort_kernel,
        in_specs=[scalar, anywhere],
        out_shape=[jax.ShapeDtypeStruct((part_rows, width), bf16)] * COARSE,
        scratch_shapes=[
            pltpu.VMEM((COARSE, inner, CHUNK, width), bf16),
            pltpu.VMEM((COARSE * inner, width), f32),
            pltpu.VMEM((inner, rows + META, width), bf16),
            pltpu.SemaphoreType.DMA((4,)),
        ],
        compiler_params=pltpu.CompilerParams(vmem_limit_bytes=24 * 2**20),
        cost_estimate=pl.CostEstimate(
            flops=2 * 10**9, bytes_accessed=3 * 2**20, transcendentals=0
        ),
    )(me, packed)
    parts = [parts[0]] + [
        lax.ppermute(parts[d], "outer", [(n, n ^ d) for n in range(outer)])
        for d in range(1, outer)
    ]

    total = devices * CAP
    by_cluster, scales = pl.pallas_call(
        queries_kernel,
        in_specs=[scalar] + [pl.BlockSpec(memory_space=pltpu.VMEM)] * COARSE,
        out_shape=[
            jax.ShapeDtypeStruct((FINE, total, width), bf16),
            jax.ShapeDtypeStruct((2 * FINE, total), f32),
        ],
        scratch_shapes=[pltpu.VMEM((devices, width), bf16)],
        cost_estimate=pl.CostEstimate(
            flops=10**9, bytes_accessed=4 * 2**20, transcendentals=0
        ),
    )(me, *parts)
    answer = pl.pallas_call(
        attend_kernel,
        in_specs=[anywhere, anywhere, pl.BlockSpec(memory_space=pltpu.VMEM)],
        out_specs=anywhere,
        out_shape=jax.ShapeDtypeStruct((devices, CHUNK, width), bf16),
        scratch_shapes=[
            pltpu.VMEM((devices, CHUNK, 2 * width), bf16),
            pltpu.VMEM((FINE, total, width), bf16),
            pltpu.VMEM((FINE, total, 2 * width), bf16),
            pltpu.VMEM((FINE, total // PIECES, width), bf16),
            pltpu.VMEM((devices, CHUNK, width), bf16),
            pltpu.SemaphoreType.DMA((3, PIECES)),
        ],
        cost_estimate=pl.CostEstimate(
            flops=4 * 10**9, bytes_accessed=8 * 2**20, transcendentals=5 * 10**6
        ),
    )(message, by_cluster, scales)
    answer = lax.all_to_all(answer, BOTH, 0, 0, tiled=True)

    return pl.pallas_call(
        unplace_kernel,
        in_specs=[pl.BlockSpec(memory_space=pltpu.VMEM), anywhere],
        out_specs=anywhere,
        out_shape=jax.ShapeDtypeStruct((rows, heads, width), bf16),
        scratch_shapes=[
            pltpu.VMEM((COARSE, heads, CHUNK, width), bf16),
            pltpu.VMEM((heads, rows, width), bf16),
            pltpu.VMEM((rows, heads, width), bf16),
            pltpu.SemaphoreType.DMA((2, PIECES)),
        ],
        compiler_params=pltpu.CompilerParams(vmem_limit_bytes=24 * 2**20),
        cost_estimate=pl.CostEstimate(
            flops=10**9, bytes_accessed=3 * 2**20, transcendentals=0
        ),
    )(slots.T, answer.reshape(COARSE, heads, CHUNK, width))


def solution(mesh):
    placed = (
        P(BOTH, None, None),
        P(BOTH, None, None),
        P(BOTH, None, None),
        P(BOTH, None),
        P(BOTH, None),
        P(None, BOTH, None),
    )
    return jax.shard_map(
        shards,
        mesh=mesh,
        in_specs=placed,
        out_specs=P(BOTH, None, None),
        check_vma=False,
    )
```

```python
import jax
import jax.numpy as jnp
from jax import lax
from jax.experimental import pallas as pl
from jax.experimental.pallas import tpu as pltpu
from jax.sharding import PartitionSpec as P

COARSE = 16
FINE = 8
CAP = 4
CLUSTERS = COARSE * FINE
SLOTS = CLUSTERS * CAP
CHUNK = FINE * CAP
META = 8
BOTH = ("outer", "inner")
NT = (((1,), (1,)), ((), ()))
NEG = -1e30
LOG2E = 1.4426950408889634
HALF = 8
PIECES = 4


def iota(shape, axis):
    return lax.broadcasted_iota(jnp.int32, shape, axis)


def one_hot(condition):
    return jnp.where(condition, 1.0, 0.0).astype(jnp.bfloat16)


def matmul(a, b):
    return jnp.dot(a, b, preferred_element_type=jnp.float32)


def matmul_nt(a, b):
    return lax.dot_general(a, b, NT, preferred_element_type=jnp.float32)


def over(x, size):
    return x >> (size.bit_length() - 1)


def rest(x, size):
    return x & (size - 1)


def swap_matrix(major, minor, unit):
    total = major * minor * unit
    row, column = iota((total, total), 0), iota((total, total), 1)
    b, a, u = over(row, major * unit), rest(over(row, unit), major), rest(row, unit)
    return one_hot(column == (a * minor + b) * unit + u)


def slot_of(label, before):
    member = iota((CLUSTERS, label.shape[1]), 0) == label
    count = matmul(one_hot(member), before)
    rank = jnp.sum(jnp.where(member, count, 0.0), axis=0, keepdims=True)
    return label * CAP + rank.astype(jnp.int32)


def before_matrix(rows):
    return one_hot(iota((rows, rows), 0) < iota((rows, rows), 1))


def pack_kernel(label_ref, key_scale_ref, value_scale_ref, q_ref, out_ref):
    rows, heads, width = q_ref.shape
    kinds = (label_ref[:, 0, :].astype(jnp.float32), key_scale_ref[...], value_scale_ref[...])
    meta = [
        kind[:, n * width : (n + 1) * width].astype(jnp.bfloat16)
        for kind in kinds
        for n in range(rows // width)
    ]
    meta.append(jnp.zeros(((META - len(meta)) * heads, width), jnp.bfloat16))
    turned = matmul(swap_matrix(META, heads, 1), jnp.concatenate(meta, axis=0))
    out_ref[:, rows : rows + META, :] = turned.astype(jnp.bfloat16).reshape(heads, META, width)
    group = 256 // heads
    swap = swap_matrix(group, heads, 1)
    for g in range(rows // group):
        block = q_ref[g * group : (g + 1) * group].reshape(256, width)
        turned = matmul(swap, block).astype(jnp.bfloat16)
        out_ref[:, g * group : (g + 1) * group, :] = turned.reshape(heads, group, width)


def place_kernel(label_ref, k_ref, v_ref, slot_ref, out_ref, by_head):
    rows, _, width = k_ref.shape
    group = 256 // HALF
    swap = swap_matrix(group, HALF, 1)
    for g in range(rows // group):
        here = slice(g * group, (g + 1) * group)
        block = jnp.concatenate(
            [k_ref[here].reshape(256, width), v_ref[here].reshape(256, width)], axis=1
        )
        turned = matmul(swap, block).astype(jnp.bfloat16)
        by_head[:, here, :] = turned.reshape(HALF, group, 2 * width)
    before = before_matrix(rows)
    for h in range(HALF):
        slot = slot_of(label_ref[h], before)
        slot_ref[h : h + 1, :] = slot
        pick = one_hot(iota((SLOTS, rows), 0) == slot)
        placed = matmul(pick, by_head[h]).astype(jnp.bfloat16)
        out_ref[:, h] = placed.reshape(COARSE, CHUNK, 2 * width)


def sort_kernel(me_ref, arrived_ref, *refs):
    outs, (table, scales, in_ref, sems) = refs[:COARSE], refs[COARSE:]
    me = me_ref[0]
    blocks, rows, width = in_ref.shape
    rows = rows - META
    batch = 256 // CHUNK
    quarter = blocks // 4
    copies = [
        pltpu.make_async_copy(
            arrived_ref.at[pl.ds(n * quarter, quarter)],
            in_ref.at[pl.ds(n * quarter, quarter)],
            sems.at[n],
        )
        for n in range(4)
    ]
    for copy in copies:
        copy.start()
    before = before_matrix(rows)
    for s in range(blocks):
        if s % quarter == 0:
            copies[s // quarter].wait()
        meta = in_ref[s, rows : rows + META, :].astype(jnp.float32)
        label, key_scale, value_scale = (
            jnp.concatenate([meta[2 * n : 2 * n + 1], meta[2 * n + 1 : 2 * n + 2]], axis=1)
            for n in range(3)
        )
        slot = slot_of(label.astype(jnp.int32), before)
        owner = over(slot, CHUNK) ^ me
        here = rest(slot, CHUNK)
        pick = one_hot(iota((SLOTS, rows), 0) == owner * CHUNK + here)
        placed = matmul(pick, in_ref[s, :rows, :]).astype(jnp.bfloat16)
        table[:, s] = placed.reshape(COARSE, CHUNK, width)
        mine = iota((CHUNK, rows), 0) == here
        both = jnp.concatenate(
            [
                jnp.where(mine, key_scale, 0.0),
                jnp.where(mine, value_scale, 0.0),
                jnp.zeros((width - 2 * CHUNK, rows), jnp.float32),
            ],
            axis=0,
        ).astype(jnp.bfloat16)
        scales[pl.ds(s, COARSE, stride=blocks), :] = matmul_nt(
            one_hot(iota((COARSE, rows), 0) == owner), both
        )
    swap = swap_matrix(batch, FINE, CAP)
    unit = batch * CAP
    for d, out_ref in enumerate(outs):
        block = jnp.concatenate(
            [
                table[d, b * batch : (b + 1) * batch].reshape(256, width)
                for b in range(blocks // batch)
            ],
            axis=1,
        )
        turned = matmul(swap, block).astype(jnp.bfloat16)
        for f in range(FINE):
            for b in range(blocks // batch):
                at = f * blocks * CAP + b * unit
                out_ref[at : at + unit, :] = turned[
                    f * unit : (f + 1) * unit, b * width : (b + 1) * width
                ]
        out_ref[FINE * blocks * CAP :, :] = scales[d * blocks : (d + 1) * blocks, :].astype(
            jnp.bfloat16
        )


def queries_kernel(me_ref, *refs):
    parts, (qs, scales, scale_rows) = refs[:COARSE], refs[COARSE:]
    me = me_ref[0]
    total, width = qs.shape[1:]
    sources = total // CAP
    blocks = sources // COARSE
    slab = blocks * CAP
    for d, part in enumerate(parts):
        source = me ^ d
        qs[:, pl.ds(pl.multiple_of(source * slab, slab), slab), :] = part[
            : FINE * slab, :
        ].reshape(FINE, slab, width)
        scale_rows[pl.ds(pl.multiple_of(source * blocks, blocks), blocks), :] = part[
            FINE * slab :, :
        ]
    spread = one_hot(over(iota((total, sources), 0), CAP) == iota((total, sources), 1))
    table = matmul(spread, scale_rows[...])
    lane, row = iota((total, 128), 1), iota((total, 128), 0)
    table = jnp.where(rest(lane, CAP) == rest(row, CAP), table, 0.0).astype(jnp.bfloat16)
    gather = one_hot(iota((2 * FINE, 128), 0) == over(iota((2 * FINE, 128), 1), CAP))
    scales[...] = matmul_nt(gather, table)


def attend_kernel(arrived_ref, q_ref, scales, out_ref, message, qs, kvs, os, result, sems):
    sources, _, width = message.shape
    width = width // 2
    piece = sources // PIECES
    tile = piece * CAP
    batch = 256 // CHUNK
    unit = batch * CAP

    def rows(n, size):
        return slice(n * size, (n + 1) * size)

    def message_in(n):
        here = pl.ds(n * piece, piece)
        return pltpu.make_async_copy(arrived_ref.at[here], message.at[here], sems.at[0, n])

    def queries_in(n):
        here = pl.ds(n * tile, tile)
        return pltpu.make_async_copy(q_ref.at[:, here], qs.at[:, here], sems.at[1, n])

    def result_out(n):
        here = pl.ds(n * piece, piece)
        return pltpu.make_async_copy(result.at[here], out_ref.at[here], sems.at[2, n])

    for n in range(PIECES):
        message_in(n).start()
        queries_in(n).start()
    turn_in = swap_matrix(batch, FINE, CAP)
    turn_out = swap_matrix(FINE, batch, CAP)
    ahead = iota((tile, tile), 1) > iota((tile, tile), 0)
    for t in range(PIECES):
        message_in(t).wait()
        for g in range(t * piece // batch, (t + 1) * piece // batch):
            block = message[rows(g, batch)].reshape(256, 2 * width)
            turned = matmul(turn_in, block).astype(jnp.bfloat16)
            kvs[:, rows(g, unit), :] = turned.reshape(FINE, unit, 2 * width)
        queries_in(t).wait()

        def scores_of(f):
            key_scale = scales[f : f + 1, :]
            factor = key_scale * (width**-0.5 * LOG2E)
            bias = jnp.where(key_scale > 0.0, 0.0, NEG)
            query = qs[f, rows(t, tile), :]
            pieces = []
            for u in range(t + 1):
                there = rows(u, tile)
                score = matmul_nt(query, kvs[f, there, :width])
                score = score * factor[:, there] + bias[:, there]
                if u == t:
                    score = jnp.where(ahead, NEG, score)
                pieces.append(score)
            return pieces

        def finish(f, pieces):
            value_scale = scales[FINE + f : FINE + f + 1, :]
            highest = pieces[0]
            for score in pieces[1:]:
                highest = jnp.maximum(highest, score)
            highest = jnp.max(highest, axis=1, keepdims=True)
            below, weights = None, []
            for u, score in enumerate(pieces):
                there = rows(u, tile)
                unnormed = jnp.exp2(score - highest)
                weights.append((unnormed * value_scale[:, there]).astype(jnp.bfloat16))
                below = unnormed if below is None else below + unnormed
            total = matmul(jnp.concatenate(weights, axis=1), kvs[f, : (t + 1) * tile, width:])
            below = jnp.sum(below, axis=1, keepdims=True)
            os[f] = (total / below).astype(jnp.bfloat16)

        upcoming = scores_of(0)
        for f in range(FINE):
            current = upcoming
            if f + 1 < FINE:
                upcoming = scores_of(f + 1)
            finish(f, current)
        for g in range(piece // batch):
            block = os[:, rows(g, unit), :].reshape(256, width)
            turned = matmul(turn_out, block).astype(jnp.bfloat16)
            result[rows(t * (piece // batch) + g, batch)] = turned.reshape(batch, CHUNK, width)
        result_out(t).start()
    for n in range(PIECES):
        result_out(n).wait()


def unplace_kernel(slot_ref, arrived_ref, out_ref, answer, by_head, result, sems):
    rows, heads, width = result.shape
    some = heads // PIECES
    piece = rows // PIECES
    group = 256 // heads

    def answer_in(n):
        here = pl.ds(n * some, some)
        return pltpu.make_async_copy(
            arrived_ref.at[:, here], answer.at[:, here], sems.at[0, n]
        )

    def result_out(n):
        here = pl.ds(n * piece, piece)
        return pltpu.make_async_copy(result.at[here], out_ref.at[here], sems.at[1, n])

    for n in range(PIECES):
        answer_in(n).start()
    place = iota((rows, SLOTS), 1)
    swap = swap_matrix(heads, group, 1)
    def pick_of(h):
        return one_hot(place == slot_ref[:, h : h + 1])

    upcoming = pick_of(0)
    for h in range(heads):
        if h % some == 0:
            answer_in(h // some).wait()
        pick = upcoming
        if h + 1 < heads:
            upcoming = pick_of(h + 1)
        by_head[h] = matmul(pick, answer[:, h].reshape(SLOTS, width)).astype(jnp.bfloat16)

    def turned(g):
        block = by_head[:, g * group : (g + 1) * group, :].reshape(256, width)
        return matmul(swap, block)

    groups = piece // group
    upcoming = turned(0)
    for g in range(rows // group):
        current = upcoming
        if (g + 1) * group < rows:
            upcoming = turned(g + 1)
        result[g * group : (g + 1) * group] = current.astype(jnp.bfloat16).reshape(
            group, heads, width
        )
        if (g + 1) % groups == 0:
            result_out(g // groups).start()
    for n in range(PIECES):
        result_out(n).wait()


def unplace_kernel(slot_ref, arrived_ref, out_ref, answer, by_head, result, sems):
    rows, heads, width = result.shape
    some = heads // PIECES
    piece = rows // PIECES
    group = 256 // heads

    def answer_in(n):
        here = pl.ds(n * some, some)
        return pltpu.make_async_copy(
            arrived_ref.at[:, here], answer.at[:, here], sems.at[0, n]
        )

    def result_out(n):
        here = pl.ds(n * piece, piece)
        return pltpu.make_async_copy(result.at[here], out_ref.at[here], sems.at[1, n])

    for n in range(PIECES):
        answer_in(n).start()
    place = iota((rows, SLOTS), 1)
    swap = swap_matrix(heads, group, 1)
    for h in range(heads):
        if h % some == 0:
            answer_in(h // some).wait()
        pick = one_hot(place == slot_ref[:, h : h + 1])
        block = answer[:, h].reshape(SLOTS, width)
        by_head[h] = matmul(pick, block).astype(jnp.bfloat16)
    for n in range(PIECES):
        for g in range(n * piece // group, (n + 1) * piece // group):
            here = slice(g * group, (g + 1) * group)
            block = by_head[:, here, :].reshape(256, width)
            result[here] = matmul(swap, block).astype(jnp.bfloat16).reshape(group, heads, width)
        result_out(n).start()
    for n in range(PIECES):
        result_out(n).wait()


def shards(queries, key_rows, value_rows, key_scale, value_scale, cluster_label):
    rows, heads, width = queries.shape
    outer, inner = lax.axis_size("outer"), lax.axis_size("inner")
    devices = outer * inner
    bf16, f32 = jnp.bfloat16, jnp.float32
    me = lax.axis_index("outer").astype(jnp.int32).reshape(1)
    scalar = pl.BlockSpec(memory_space=pltpu.SMEM)

    anywhere = pl.BlockSpec(memory_space=pl.ANY)
    labels = jnp.swapaxes(cluster_label, 1, 2)
    packed = pl.pallas_call(
        pack_kernel,
        out_shape=jax.ShapeDtypeStruct((heads, rows + META, width), bf16),
        cost_estimate=pl.CostEstimate(flops=10**9, bytes_accessed=2**21, transcendentals=0),
    )(labels, key_scale.T, value_scale.T, queries)
    packed = lax.all_to_all(packed, "inner", 0, 0, tiled=True)

    tokens = pl.BlockSpec((rows, HALF, width), lambda i: (0, i, 0))
    slots, message = pl.pallas_call(
        place_kernel,
        grid=(heads // HALF,),
        in_specs=[pl.BlockSpec((HALF, 1, rows), lambda i: (i, 0, 0)), tokens, tokens],
        out_specs=[
            pl.BlockSpec((HALF, rows), lambda i: (i, 0)),
            pl.BlockSpec((COARSE, HALF, CHUNK, 2 * width), lambda i: (0, i, 0, 0)),
        ],
        out_shape=[
            jax.ShapeDtypeStruct((heads, rows), jnp.int32),
            jax.ShapeDtypeStruct((COARSE, heads, CHUNK, 2 * width), bf16),
        ],
        scratch_shapes=[pltpu.VMEM((HALF, rows, 2 * width), bf16)],
        cost_estimate=pl.CostEstimate(
            flops=3 * 10**9, bytes_accessed=6 * 2**20, transcendentals=0
        ),
    )(labels, key_rows, value_rows)
    message = message.reshape(devices, CHUNK, 2 * width)
    message = lax.all_to_all(message, BOTH, 0, 0, tiled=True)

    part_rows = FINE * inner * CAP + inner
    parts = pl.pallas_call(
        sort_kernel,
        in_specs=[scalar, anywhere],
        out_shape=[jax.ShapeDtypeStruct((part_rows, width), bf16)] * COARSE,
        scratch_shapes=[
            pltpu.VMEM((COARSE, inner, CHUNK, width), bf16),
            pltpu.VMEM((COARSE * inner, width), f32),
            pltpu.VMEM((inner, rows + META, width), bf16),
            pltpu.SemaphoreType.DMA((4,)),
        ],
        compiler_params=pltpu.CompilerParams(vmem_limit_bytes=24 * 2**20),
        cost_estimate=pl.CostEstimate(
            flops=2 * 10**9, bytes_accessed=3 * 2**20, transcendentals=0
        ),
    )(me, packed)
    parts = [parts[0]] + [
        lax.ppermute(parts[d], "outer", [(n, n ^ d) for n in range(outer)])
        for d in range(1, outer)
    ]

    total = devices * CAP
    by_cluster, scales = pl.pallas_call(
        queries_kernel,
        in_specs=[scalar] + [pl.BlockSpec(memory_space=pltpu.VMEM)] * COARSE,
        out_shape=[
            jax.ShapeDtypeStruct((FINE, total, width), bf16),
            jax.ShapeDtypeStruct((2 * FINE, total), f32),
        ],
        scratch_shapes=[pltpu.VMEM((devices, width), bf16)],
        cost_estimate=pl.CostEstimate(
            flops=10**9, bytes_accessed=4 * 2**20, transcendentals=0
        ),
    )(me, *parts)
    answer = pl.pallas_call(
        attend_kernel,
        in_specs=[anywhere, anywhere, pl.BlockSpec(memory_space=pltpu.VMEM)],
        out_specs=anywhere,
        out_shape=jax.ShapeDtypeStruct((devices, CHUNK, width), bf16),
        scratch_shapes=[
            pltpu.VMEM((devices, CHUNK, 2 * width), bf16),
            pltpu.VMEM((FINE, total, width), bf16),
            pltpu.VMEM((FINE, total, 2 * width), bf16),
            pltpu.VMEM((FINE, total // PIECES, width), bf16),
            pltpu.VMEM((devices, CHUNK, width), bf16),
            pltpu.SemaphoreType.DMA((3, PIECES)),
        ],
        cost_estimate=pl.CostEstimate(
            flops=4 * 10**9, bytes_accessed=8 * 2**20, transcendentals=5 * 10**6
        ),
    )(message, by_cluster, scales)
    answer = lax.all_to_all(answer, BOTH, 0, 0, tiled=True)

    return pl.pallas_call(
        unplace_kernel,
        in_specs=[pl.BlockSpec(memory_space=pltpu.VMEM), anywhere],
        out_specs=anywhere,
        out_shape=jax.ShapeDtypeStruct((rows, heads, width), bf16),
        scratch_shapes=[
            pltpu.VMEM((COARSE, heads, CHUNK, width), bf16),
            pltpu.VMEM((heads, rows, width), bf16),
            pltpu.VMEM((rows, heads, width), bf16),
            pltpu.SemaphoreType.DMA((2, PIECES)),
        ],
        compiler_params=pltpu.CompilerParams(vmem_limit_bytes=24 * 2**20),
        cost_estimate=pl.CostEstimate(
            flops=10**9, bytes_accessed=3 * 2**20, transcendentals=0
        ),
    )(slots.T, answer.reshape(COARSE, heads, CHUNK, width))


def solution(mesh):
    placed = (
        P(BOTH, None, None),
        P(BOTH, None, None),
        P(BOTH, None, None),
        P(BOTH, None),
        P(BOTH, None),
        P(None, BOTH, None),
    )
    return jax.shard_map(
        shards,
        mesh=mesh,
        in_specs=placed,
        out_specs=P(BOTH, None, None),
        check_vma=False,
    )
```

```python
import jax
import jax.numpy as jnp
from jax import lax
from jax.experimental import pallas as pl
from jax.experimental.pallas import tpu as pltpu
from jax.sharding import PartitionSpec as P

COARSE = 16
FINE = 8
CAP = 4
CLUSTERS = COARSE * FINE
SLOTS = CLUSTERS * CAP
CHUNK = FINE * CAP
META = 8
BOTH = ("outer", "inner")
NT = (((1,), (1,)), ((), ()))
NEG = -1e30
LOG2E = 1.4426950408889634
HALF = 8
PIECES = 4


def iota(shape, axis):
    return lax.broadcasted_iota(jnp.int32, shape, axis)


def one_hot(condition):
    return jnp.where(condition, 1.0, 0.0).astype(jnp.bfloat16)


def matmul(a, b):
    return jnp.dot(a, b, preferred_element_type=jnp.float32)


def matmul_nt(a, b):
    return lax.dot_general(a, b, NT, preferred_element_type=jnp.float32)


def over(x, size):
    return x >> (size.bit_length() - 1)


def rest(x, size):
    return x & (size - 1)


def swap_matrix(major, minor, unit):
    total = major * minor * unit
    row, column = iota((total, total), 0), iota((total, total), 1)
    b, a, u = over(row, major * unit), rest(over(row, unit), major), rest(row, unit)
    return one_hot(column == (a * minor + b) * unit + u)


def slot_of(label, before):
    member = iota((CLUSTERS, label.shape[1]), 0) == label
    count = matmul(one_hot(member), before)
    rank = jnp.sum(jnp.where(member, count, 0.0), axis=0, keepdims=True)
    return label * CAP + rank.astype(jnp.int32)


def before_matrix(rows):
    return one_hot(iota((rows, rows), 0) < iota((rows, rows), 1))


def pack_kernel(label_ref, key_scale_ref, value_scale_ref, q_ref, out_ref):
    rows, heads, width = q_ref.shape
    kinds = (label_ref[:, 0, :].astype(jnp.float32), key_scale_ref[...], value_scale_ref[...])
    meta = [
        kind[:, n * width : (n + 1) * width].astype(jnp.float32)
        for kind in kinds
        for n in range(rows // width)
    ]
    meta.append(jnp.zeros(((META - len(meta)) * heads, width), jnp.float32))
    meta = jnp.concatenate(meta, axis=0).astype(jnp.bfloat16)
    turned = matmul(swap_matrix(META, heads, 1), meta)
    out_ref[:, rows : rows + META, :] = turned.astype(jnp.bfloat16).reshape(heads, META, width)
    group = 256 // heads
    swap = swap_matrix(group, heads, 1)
    for g in range(rows // group):
        block = q_ref[g * group : (g + 1) * group].reshape(256, width)
        turned = matmul(swap, block).astype(jnp.bfloat16)
        out_ref[:, g * group : (g + 1) * group, :] = turned.reshape(heads, group, width)


def place_kernel(label_ref, k_ref, v_ref, slot_ref, out_ref, by_head):
    rows, _, width = k_ref.shape
    group = 256 // HALF
    swap = swap_matrix(group, HALF, 1)
    for g in range(rows // group):
        here = slice(g * group, (g + 1) * group)
        block = jnp.concatenate(
            [k_ref[here].reshape(256, width), v_ref[here].reshape(256, width)], axis=1
        )
        turned = matmul(swap, block).astype(jnp.bfloat16)
        by_head[:, here, :] = turned.reshape(HALF, group, 2 * width)
    before = before_matrix(rows)
    for h in range(HALF):
        slot = slot_of(label_ref[h], before)
        slot_ref[h : h + 1, :] = slot
        pick = one_hot(iota((SLOTS, rows), 0) == slot)
        placed = matmul(pick, by_head[h]).astype(jnp.bfloat16)
        out_ref[:, h] = placed.reshape(COARSE, CHUNK, 2 * width)


def sort_kernel(me_ref, arrived_ref, *refs):
    outs, (table, scales, in_ref, sems) = refs[:COARSE], refs[COARSE:]
    me = me_ref[0]
    blocks, rows, width = in_ref.shape
    rows = rows - META
    batch = 256 // CHUNK
    quarter = blocks // 4
    copies = [
        pltpu.make_async_copy(
            arrived_ref.at[pl.ds(n * quarter, quarter)],
            in_ref.at[pl.ds(n * quarter, quarter)],
            sems.at[n],
        )
        for n in range(4)
    ]
    for copy in copies:
        copy.start()
    before = before_matrix(rows)
    for s in range(blocks):
        if s % quarter == 0:
            copies[s // quarter].wait()
        meta = in_ref[s, rows : rows + META, :].astype(jnp.float32)
        label, key_scale, value_scale = (
            jnp.concatenate([meta[2 * n : 2 * n + 1], meta[2 * n + 1 : 2 * n + 2]], axis=1)
            for n in range(3)
        )
        slot = slot_of(label.astype(jnp.int32), before)
        owner = over(slot, CHUNK) ^ me
        here = rest(slot, CHUNK)
        pick = one_hot(iota((SLOTS, rows), 0) == owner * CHUNK + here)
        placed = matmul(pick, in_ref[s, :rows, :]).astype(jnp.bfloat16)
        table[:, s] = placed.reshape(COARSE, CHUNK, width)
        mine = iota((CHUNK, rows), 0) == here
        both = jnp.concatenate(
            [
                jnp.where(mine, key_scale, 0.0),
                jnp.where(mine, value_scale, 0.0),
                jnp.zeros((width - 2 * CHUNK, rows), jnp.float32),
            ],
            axis=0,
        ).astype(jnp.bfloat16)
        scales[pl.ds(s, COARSE, stride=blocks), :] = matmul_nt(
            one_hot(iota((COARSE, rows), 0) == owner), both
        )
    swap = swap_matrix(batch, FINE, CAP)
    unit = batch * CAP
    for d, out_ref in enumerate(outs):
        block = jnp.concatenate(
            [
                table[d, b * batch : (b + 1) * batch].reshape(256, width)
                for b in range(blocks // batch)
            ],
            axis=1,
        )
        turned = matmul(swap, block).astype(jnp.bfloat16)
        for f in range(FINE):
            for b in range(blocks // batch):
                at = f * blocks * CAP + b * unit
                out_ref[at : at + unit, :] = turned[
                    f * unit : (f + 1) * unit, b * width : (b + 1) * width
                ]
        out_ref[FINE * blocks * CAP :, :] = scales[d * blocks : (d + 1) * blocks, :].astype(
            jnp.bfloat16
        )


def queries_kernel(me_ref, *refs):
    parts, (qs, scales, scale_rows) = refs[:COARSE], refs[COARSE:]
    me = me_ref[0]
    total, width = qs.shape[1:]
    sources = total // CAP
    blocks = sources // COARSE
    slab = blocks * CAP
    for d, part in enumerate(parts):
        source = me ^ d
        qs[:, pl.ds(pl.multiple_of(source * slab, slab), slab), :] = part[
            : FINE * slab, :
        ].reshape(FINE, slab, width)
        scale_rows[pl.ds(pl.multiple_of(source * blocks, blocks), blocks), :] = part[
            FINE * slab :, :
        ]
    spread = one_hot(over(iota((total, sources), 0), CAP) == iota((total, sources), 1))
    table = matmul(spread, scale_rows[...])
    lane, row = iota((total, 128), 1), iota((total, 128), 0)
    table = jnp.where(rest(lane, CAP) == rest(row, CAP), table, 0.0).astype(jnp.bfloat16)
    gather = one_hot(iota((2 * FINE, 128), 0) == over(iota((2 * FINE, 128), 1), CAP))
    scales[...] = matmul_nt(gather, table)


def attend_kernel(arrived_ref, q_ref, scales, out_ref, message, qs, kvs, os, result, sems):
    sources, _, width = message.shape
    width = width // 2
    piece = sources // PIECES
    tile = piece * CAP
    batch = 256 // CHUNK
    unit = batch * CAP

    def rows(n, size):
        return slice(n * size, (n + 1) * size)

    def message_in(n):
        here = pl.ds(n * piece, piece)
        return pltpu.make_async_copy(arrived_ref.at[here], message.at[here], sems.at[0, n])

    def queries_in(n):
        here = pl.ds(n * tile, tile)
        return pltpu.make_async_copy(q_ref.at[:, here], qs.at[:, here], sems.at[1, n])

    def result_out(n):
        here = pl.ds(n * piece, piece)
        return pltpu.make_async_copy(result.at[here], out_ref.at[here], sems.at[2, n])

    for n in range(PIECES):
        message_in(n).start()
        queries_in(n).start()
    turn_in = swap_matrix(batch, FINE, CAP)
    turn_out = swap_matrix(FINE, batch, CAP)
    ahead = iota((tile, tile), 1) > iota((tile, tile), 0)
    for t in range(PIECES):
        message_in(t).wait()
        for g in range(t * piece // batch, (t + 1) * piece // batch):
            block = message[rows(g, batch)].reshape(256, 2 * width)
            turned = matmul(turn_in, block).astype(jnp.bfloat16)
            kvs[:, rows(g, unit), :] = turned.reshape(FINE, unit, 2 * width)
        queries_in(t).wait()

        def scores_of(f):
            key_scale = scales[f : f + 1, :]
            factor = key_scale * (width**-0.5 * LOG2E)
            bias = jnp.where(key_scale > 0.0, 0.0, NEG)
            query = qs[f, rows(t, tile), :]
            pieces = []
            for u in range(t + 1):
                there = rows(u, tile)
                score = matmul_nt(query, kvs[f, there, :width])
                score = score * factor[:, there] + bias[:, there]
                if u == t:
                    score = jnp.where(ahead, NEG, score)
                pieces.append(score)
            return pieces

        def finish(f, pieces):
            value_scale = scales[FINE + f : FINE + f + 1, :]
            highest = pieces[0]
            for score in pieces[1:]:
                highest = jnp.maximum(highest, score)
            highest = jnp.max(highest, axis=1, keepdims=True)
            below, weights = None, []
            for u, score in enumerate(pieces):
                there = rows(u, tile)
                unnormed = jnp.exp2(score - highest)
                weights.append((unnormed * value_scale[:, there]).astype(jnp.bfloat16))
                below = unnormed if below is None else below + unnormed
            total = matmul(jnp.concatenate(weights, axis=1), kvs[f, : (t + 1) * tile, width:])
            below = jnp.sum(below, axis=1, keepdims=True)
            os[f] = (total / below).astype(jnp.bfloat16)

        upcoming = scores_of(0)
        for f in range(FINE):
            current = upcoming
            if f + 1 < FINE:
                upcoming = scores_of(f + 1)
            finish(f, current)
        for g in range(piece // batch):
            block = os[:, rows(g, unit), :].reshape(256, width)
            turned = matmul(turn_out, block).astype(jnp.bfloat16)
            result[rows(t * (piece // batch) + g, batch)] = turned.reshape(batch, CHUNK, width)
        result_out(t).start()
    for n in range(PIECES):
        result_out(n).wait()


def unplace_kernel(slot_ref, arrived_ref, out_ref, answer, by_head, result, sems):
    rows, heads, width = result.shape
    some = heads // PIECES
    piece = rows // PIECES
    group = 256 // heads

    def answer_in(n):
        here = pl.ds(n * some, some)
        return pltpu.make_async_copy(
            arrived_ref.at[:, here], answer.at[:, here], sems.at[0, n]
        )

    def result_out(n):
        here = pl.ds(n * piece, piece)
        return pltpu.make_async_copy(result.at[here], out_ref.at[here], sems.at[1, n])

    for n in range(PIECES):
        answer_in(n).start()
    place = iota((rows, SLOTS), 1)
    swap = swap_matrix(heads, group, 1)
    def pick_of(h):
        return one_hot(place == slot_ref[:, h : h + 1])

    upcoming = pick_of(0)
    for h in range(heads):
        if h % some == 0:
            answer_in(h // some).wait()
        pick = upcoming
        if h + 1 < heads:
            upcoming = pick_of(h + 1)
        by_head[h] = matmul(pick, answer[:, h].reshape(SLOTS, width)).astype(jnp.bfloat16)

    def turned(g):
        block = by_head[:, g * group : (g + 1) * group, :].reshape(256, width)
        return matmul(swap, block)

    groups = piece // group
    upcoming = turned(0)
    for g in range(rows // group):
        current = upcoming
        if (g + 1) * group < rows:
            upcoming = turned(g + 1)
        result[g * group : (g + 1) * group] = current.astype(jnp.bfloat16).reshape(
            group, heads, width
        )
        if (g + 1) % groups == 0:
            result_out(g // groups).start()
    for n in range(PIECES):
        result_out(n).wait()


def unplace_kernel(slot_ref, arrived_ref, out_ref, answer, by_head, result, sems):
    rows, heads, width = result.shape
    some = heads // PIECES
    piece = rows // PIECES
    group = 256 // heads

    def answer_in(n):
        here = pl.ds(n * some, some)
        return pltpu.make_async_copy(
            arrived_ref.at[:, here], answer.at[:, here], sems.at[0, n]
        )

    def result_out(n):
        here = pl.ds(n * piece, piece)
        return pltpu.make_async_copy(result.at[here], out_ref.at[here], sems.at[1, n])

    for n in range(PIECES):
        answer_in(n).start()
    place = iota((rows, SLOTS), 1)
    swap = swap_matrix(heads, group, 1)
    for h in range(heads):
        if h % some == 0:
            answer_in(h // some).wait()
        pick = one_hot(place == slot_ref[:, h : h + 1])
        block = answer[:, h].reshape(SLOTS, width)
        by_head[h] = matmul(pick, block).astype(jnp.bfloat16)
    for n in range(PIECES):
        for g in range(n * piece // group, (n + 1) * piece // group):
            here = slice(g * group, (g + 1) * group)
            block = by_head[:, here, :].reshape(256, width)
            result[here] = matmul(swap, block).astype(jnp.bfloat16).reshape(group, heads, width)
        result_out(n).start()
    for n in range(PIECES):
        result_out(n).wait()


def shards(queries, key_rows, value_rows, key_scale, value_scale, cluster_label):
    rows, heads, width = queries.shape
    outer, inner = lax.axis_size("outer"), lax.axis_size("inner")
    devices = outer * inner
    bf16, f32 = jnp.bfloat16, jnp.float32
    me = lax.axis_index("outer").astype(jnp.int32).reshape(1)
    scalar = pl.BlockSpec(memory_space=pltpu.SMEM)

    anywhere = pl.BlockSpec(memory_space=pl.ANY)
    labels = jnp.swapaxes(cluster_label, 1, 2)
    packed = pl.pallas_call(
        pack_kernel,
        grid=(heads // HALF,),
        in_specs=[
            pl.BlockSpec((HALF, 1, rows), lambda i: (i, 0, 0)),
            pl.BlockSpec((HALF, rows), lambda i: (i, 0)),
            pl.BlockSpec((HALF, rows), lambda i: (i, 0)),
            pl.BlockSpec((rows, HALF, width), lambda i: (0, i, 0)),
        ],
        out_specs=pl.BlockSpec((HALF, rows + META, width), lambda i: (i, 0, 0)),
        out_shape=jax.ShapeDtypeStruct((heads, rows + META, width), bf16),
        cost_estimate=pl.CostEstimate(flops=10**9, bytes_accessed=2**21, transcendentals=0),
    )(labels, key_scale.T, value_scale.T, queries)
    packed = lax.all_to_all(packed, "inner", 0, 0, tiled=True)

    tokens = pl.BlockSpec((rows, HALF, width), lambda i: (0, i, 0))
    slots, message = pl.pallas_call(
        place_kernel,
        grid=(heads // HALF,),
        in_specs=[pl.BlockSpec((HALF, 1, rows), lambda i: (i, 0, 0)), tokens, tokens],
        out_specs=[
            pl.BlockSpec((HALF, rows), lambda i: (i, 0)),
            pl.BlockSpec((COARSE, HALF, CHUNK, 2 * width), lambda i: (0, i, 0, 0)),
        ],
        out_shape=[
            jax.ShapeDtypeStruct((heads, rows), jnp.int32),
            jax.ShapeDtypeStruct((COARSE, heads, CHUNK, 2 * width), bf16),
        ],
        scratch_shapes=[pltpu.VMEM((HALF, rows, 2 * width), bf16)],
        cost_estimate=pl.CostEstimate(
            flops=3 * 10**9, bytes_accessed=6 * 2**20, transcendentals=0
        ),
    )(labels, key_rows, value_rows)
    message = message.reshape(devices, CHUNK, 2 * width)
    message = lax.all_to_all(message, BOTH, 0, 0, tiled=True)

    part_rows = FINE * inner * CAP + inner
    parts = pl.pallas_call(
        sort_kernel,
        in_specs=[scalar, anywhere],
        out_shape=[jax.ShapeDtypeStruct((part_rows, width), bf16)] * COARSE,
        scratch_shapes=[
            pltpu.VMEM((COARSE, inner, CHUNK, width), bf16),
            pltpu.VMEM((COARSE * inner, width), f32),
            pltpu.VMEM((inner, rows + META, width), bf16),
            pltpu.SemaphoreType.DMA((4,)),
        ],
        compiler_params=pltpu.CompilerParams(vmem_limit_bytes=24 * 2**20),
        cost_estimate=pl.CostEstimate(
            flops=2 * 10**9, bytes_accessed=3 * 2**20, transcendentals=0
        ),
    )(me, packed)
    parts = [parts[0]] + [
        lax.ppermute(parts[d], "outer", [(n, n ^ d) for n in range(outer)])
        for d in range(1, outer)
    ]

    total = devices * CAP
    by_cluster, scales = pl.pallas_call(
        queries_kernel,
        in_specs=[scalar] + [pl.BlockSpec(memory_space=pltpu.VMEM)] * COARSE,
        out_shape=[
            jax.ShapeDtypeStruct((FINE, total, width), bf16),
            jax.ShapeDtypeStruct((2 * FINE, total), f32),
        ],
        scratch_shapes=[pltpu.VMEM((devices, width), bf16)],
        cost_estimate=pl.CostEstimate(
            flops=10**9, bytes_accessed=4 * 2**20, transcendentals=0
        ),
    )(me, *parts)
    answer = pl.pallas_call(
        attend_kernel,
        in_specs=[anywhere, anywhere, pl.BlockSpec(memory_space=pltpu.VMEM)],
        out_specs=anywhere,
        out_shape=jax.ShapeDtypeStruct((devices, CHUNK, width), bf16),
        scratch_shapes=[
            pltpu.VMEM((devices, CHUNK, 2 * width), bf16),
            pltpu.VMEM((FINE, total, width), bf16),
            pltpu.VMEM((FINE, total, 2 * width), bf16),
            pltpu.VMEM((FINE, total // PIECES, width), bf16),
            pltpu.VMEM((devices, CHUNK, width), bf16),
            pltpu.SemaphoreType.DMA((3, PIECES)),
        ],
        cost_estimate=pl.CostEstimate(
            flops=4 * 10**9, bytes_accessed=8 * 2**20, transcendentals=5 * 10**6
        ),
    )(message, by_cluster, scales)
    answer = lax.all_to_all(answer, BOTH, 0, 0, tiled=True)

    return pl.pallas_call(
        unplace_kernel,
        in_specs=[pl.BlockSpec(memory_space=pltpu.VMEM), anywhere],
        out_specs=anywhere,
        out_shape=jax.ShapeDtypeStruct((rows, heads, width), bf16),
        scratch_shapes=[
            pltpu.VMEM((COARSE, heads, CHUNK, width), bf16),
            pltpu.VMEM((heads, rows, width), bf16),
            pltpu.VMEM((rows, heads, width), bf16),
            pltpu.SemaphoreType.DMA((2, PIECES)),
        ],
        compiler_params=pltpu.CompilerParams(vmem_limit_bytes=24 * 2**20),
        cost_estimate=pl.CostEstimate(
            flops=10**9, bytes_accessed=3 * 2**20, transcendentals=0
        ),
    )(slots.T, answer.reshape(COARSE, heads, CHUNK, width))


def solution(mesh):
    placed = (
        P(BOTH, None, None),
        P(BOTH, None, None),
        P(BOTH, None, None),
        P(BOTH, None),
        P(BOTH, None),
        P(None, BOTH, None),
    )
    return jax.shard_map(
        shards,
        mesh=mesh,
        in_specs=placed,
        out_specs=P(BOTH, None, None),
        check_vma=False,
    )
```
